32 devices in a mesh: prow: 4 (over z), pcol: 8 (over y, x, core).
Axes of the slice: x: 2, y: 2, z: 4, core: 2. Of those that a mesh axis runs over, the one named last changes fastest.
Arguments:
- anc_inverse: float32 [2048, 2048], P('pcol', 'prow')
- pattern_one: int32 [8, 4], replicated, may hold values from 0 to 7, as said below
- parents: int32 [8], replicated, may hold values from 0 to 7, as said below
- low_one: float32 [8, 1024, 256], P('pcol', 'prow'), may hold values from -2 to 2
- pivot_one: float32 [8, 256, 256], P('pcol'), may hold values from -4 to 4
- low_two: float32 [8, 1024, 256], P('pcol', 'prow'), may hold values from -2 to 2
- second_scaled_factor: float32 [8, 256, 256], P('pcol'), may hold values from -2 to 2
- second_pivot_inverse: float32 [8, 256, 256], P('pcol'), may hold values from -4 to 4
Outputs:
- column_one: float32 [8, 2048, 256], P('prow', 'pcol')
- diag_one: float32 [8, 256, 256], P('pcol')
- column_two: float32 [8, 2048, 256], P('prow', 'pcol')
- second_parent_inverse: float32 [8, 256, 256], P('pcol')
- second_diagonal_inverse: float32 [8, 256, 256], P('pcol')
The draws below stay inside these ranges and needn't reach their ends.
Inputs may be any that keep to these rules, and one draw needn't show every extreme that they name: `pattern_one`: entry r of each row names an ancestor of process row r: it lies in r * 2 to r * 2 + 1; for each r, every ancestor of that range is entry r of exactly 4 rows. `parents`: every first-level supernode is the parent of exactly one second-level supernode.
All inputs are finite; a program needn't handle non-finite values.
Results may differ from the reference program's by a relative error of at most 0.000073.
Values sent between devices are 32-bit elements; how exact they have to be, the bound alone decides.
A program may use at most 128 MiB of HBM per device.

```python
import jax
import jax.numpy as jnp
from jax import lax

B = 256
NA = 8
P_SIZE = 4
CB = 2
K1 = 8
M2 = 8


def draw_anc_inverse(key, part):
    total = NA * B
    noise = jax.random.normal(key, (total, total), jnp.float32)
    symmetric = (noise + noise.T) * (0.35 / jnp.sqrt(2.0 * total))
    return jnp.eye(total, dtype=jnp.float32) + symmetric


def draw_pattern_one(key, part):
    column_keys = jax.random.split(jax.random.fold_in(key, 17), P_SIZE)
    base = (jnp.arange(K1, dtype=jnp.int32) % CB).astype(jnp.int32)
    offsets = jax.vmap(lambda k: jax.random.permutation(k, base))(column_keys).T
    starts = jnp.arange(P_SIZE, dtype=jnp.int32)[None, :] * CB
    return (offsets + starts).astype(jnp.int32)


def draw_parents(key, part):
    base = (jnp.arange(M2, dtype=jnp.int32) % K1).astype(jnp.int32)
    return jax.random.permutation(jax.random.fold_in(key, 29), base).astype(jnp.int32)


def block_levels(rng, shape, cuts, least, high):
    def one(position, shards_of):
        heights = jax.random.uniform(jax.random.fold_in(jax.random.fold_in(rng, 6), position), (shards_of,), jnp.float32, least / len(cuts), high / len(cuts))
        return jnp.repeat(jnp.exp(heights), shape[position] // shards_of).reshape((-1,) + (1,) * (len(shape) - position - 1))

    gain = one(*cuts[0])
    for cut in cuts[1:]:
        gain = gain * one(*cut)
    return gain


def gaussian(key, dims, scale, limit, cuts=(), kind=jnp.bfloat16):
    result = scale * jax.random.normal(key, dims, jnp.float32)
    if cuts:
        result = result * block_levels(key, dims, cuts, -0.22, 0.18)
    return jnp.clip(result, -limit, limit).astype(kind)


def setup_inputs(seed: int = 0) -> dict:
    splits = jax.random.split(jax.random.key(seed), 9)
    anc_inverse = draw_anc_inverse(jax.random.fold_in(splits[8], 71), 0)
    pattern_one = draw_pattern_one(jax.random.fold_in(splits[8], 71), 0)
    parents = draw_parents(jax.random.fold_in(splits[8], 71), 0)
    low_one = gaussian(splits[3], (K1, P_SIZE * B, B), 0.15, 2.0, ((0, 8), (1, 4)), jnp.float32)
    pivot_one = gaussian(splits[4], (K1, B, B), 0.3, 4.0, ((0, 8),), jnp.float32)
    low_two = gaussian(splits[5], (M2, P_SIZE * B, B), 0.15, 2.0, ((0, 8), (1, 4)), jnp.float32)
    second_scaled_factor = gaussian(splits[6], (M2, B, B), 0.15, 2.0, ((0, 8),), jnp.float32)
    second_pivot_inverse = gaussian(splits[7], (M2, B, B), 0.3, 4.0, ((0, 8),), jnp.float32)
    return {"anc_inverse": anc_inverse, "pattern_one": pattern_one, "parents": parents, "low_one": low_one, "pivot_one": pivot_one, "low_two": low_two, "second_scaled_factor": second_scaled_factor, "second_pivot_inverse": second_pivot_inverse}


def reference(anc_inverse, pattern_one, parents, low_one, pivot_one, low_two, second_scaled_factor, second_pivot_inverse):
    highest_accuracy = lax.Precision.HIGHEST
    blocks = anc_inverse.reshape(NA, B, NA, B).transpose(0, 2, 1, 3)
    lower_one = low_one.reshape(K1, P_SIZE, B, B)
    lower_two = low_two.reshape(M2, P_SIZE, B, B)

    def first_column(args):
        slots, factor = args
        chosen = blocks[:, slots]
        return -jnp.einsum('iprs,pst->irt', chosen, factor, precision=highest_accuracy)

    column_full = lax.map(first_column, (pattern_one, lower_one))
    on_slots = jax.vmap(lambda z, s: z[s])(column_full, pattern_one)
    diag_one = pivot_one - jnp.einsum('kpsa,kpsb->kab', lower_one, on_slots, precision=highest_accuracy)

    pattern_two = pattern_one[parents]
    parent_column = column_full[parents]

    def second_column(args):
        slots, factor, upper, parent_block = args
        chosen = blocks[:, slots]
        local_sum = jnp.einsum('iprs,pst->irt', chosen, factor, precision=highest_accuracy)
        carried = jnp.einsum('irs,st->irt', parent_block, upper, precision=highest_accuracy)
        return -(carried + local_sum)

    column_two_full = lax.map(second_column, (pattern_two, lower_two, second_scaled_factor, parent_column))
    parent_slots = on_slots[parents]
    second_parent_inverse = -(jnp.einsum('mab,mbd->mad', diag_one[parents], second_scaled_factor, precision=highest_accuracy)
                  + jnp.einsum('mpsa,mpsb->mab', parent_slots, lower_two, precision=highest_accuracy))
    second_on_slots = jax.vmap(lambda z, s: z[s])(column_two_full, pattern_two)
    second_diagonal_inverse = (second_pivot_inverse - jnp.einsum('oik,oiu->oku', second_scaled_factor, second_parent_inverse, precision=highest_accuracy)
                - jnp.einsum('mpsa,mpsb->mab', lower_two, second_on_slots, precision=highest_accuracy))
    column_one = column_full.reshape(K1, NA * B, B)
    column_two = column_two_full.reshape(M2, NA * B, B)
    return (column_one, diag_one, column_two, second_parent_inverse, second_diagonal_inverse)
```

```python
import functools

import jax
import jax.numpy as jnp
from jax import lax
from jax.experimental import pallas as pl
from jax.experimental.pallas import tpu as pltpu
from jax.sharding import PartitionSpec as P

MESH = pl.DeviceIdType.MESH
CORES = 2
UP, DOWN = 0, 1
LOW_ONE, LOW_TWO, LOW_PARENT = 0, 1, 2
DIAG, CROSS, SECOND = 0, 1, 2
KINDS = 3


def split(x):
    hi = x.astype(jnp.bfloat16)
    return hi, (x - hi.astype(jnp.float32)).astype(jnp.bfloat16)


def dot3(left, right, transposed=False):
    contract = (((0,), (0,)), ((), ())) if transposed else (((1,), (0,)), ((), ()))
    dot = functools.partial(
        lax.dot_general, dimension_numbers=contract, preferred_element_type=jnp.float32
    )
    return dot(left[0], right[1]) + dot(left[1], right[0]) + dot(left[0], right[0])


def fused_kernel(
    rows,
    cols,
    pattern,
    parents,
    anc,
    low_one,
    pivot_one,
    low_two,
    factor,
    pivot_two,
    out_one,
    out_diag,
    out_two,
    out_cross,
    out_second,
    z,
    low,
    whole_factor,
    scattered,
    scattered_pivot,
    scattered_two,
    staged,
    pivot_own,
    pivot_second,
    sums,
    column,
    parent_column,
    product,
    column_two,
    partial,
    partials,
    reduced,
    final,
    load_sem,
    scatter_send,
    scatter_recv,
    factor_send,
    factor_recv,
    swap_send,
    swap_recv,
    low_send,
    low_recv,
    share_send,
    share_recv,
    z_send,
    z_recv,
    near_send,
    near_recv,
    column_send,
    column_recv,
    column_store,
    part_send,
    part_recv,
    line_send,
    line_recv,
    last_send,
    last_recv,
):
    row, col = lax.axis_index("prow"), lax.axis_index("pcol")
    chips = cols // CORES
    width = factor.shape[1]
    piece = width // chips
    owned = anc.shape[1] // width
    chip, core = col // CORES, lax.rem(col, CORES)
    other = 1 - core
    mine = row * CORES + core
    partner = (row, chip * CORES + other)

    def beside(p):
        return (row, p * CORES + core)

    def turn(start, d, size):
        return lax.rem(start + d + size, size)

    def rows_of(p):
        return pl.ds(pl.multiple_of(p * piece, piece), piece)

    def remote(source, target, send, recv, device):
        return pltpu.make_async_remote_copy(
            src_ref=source,
            dst_ref=target,
            send_sem=send,
            recv_sem=recv,
            device_id=device,
            device_id_type=MESH,
        )

    def order(t):
        below, above = row, rows - 1 - row
        both = 2 * jnp.minimum(below, above)
        paired = t <= both
        distance = jnp.where(paired, (t + 1) // 2, t - both // 2)
        up = jnp.where(paired, lax.rem(t, 2) == 1, above > below)
        return jnp.where(up, row + distance, row - distance)

    sent = []

    loads = [
        pltpu.make_async_copy(
            anc.at[:, pl.ds(b * width, width)], z.at[row, core, b], load_sem.at[b]
        )
        for b in range(owned)
    ]
    loads_low = [
        pltpu.make_async_copy(
            low_one.at[0, rows_of(chip)], scattered.at[core, chip], load_sem.at[owned]
        ),
        pltpu.make_async_copy(
            low_two.at[0, rows_of(chip)], scattered_two.at[chip], load_sem.at[owned + 1]
        ),
        pltpu.make_async_copy(
            pivot_one.at[0, rows_of(chip)], scattered_pivot.at[core, chip], load_sem.at[owned + 2]
        ),
    ]
    loads_last = [
        pltpu.make_async_copy(pivot_one.at[0], pivot_own, load_sem.at[owned + 3]),
        pltpu.make_async_copy(pivot_two.at[0], pivot_second, load_sem.at[owned + 4]),
    ]
    load_factor = pltpu.make_async_copy(factor.at[0], whole_factor, load_sem.at[owned + 5])
    for copy in loads + loads_low + loads_last:
        copy.start()

    @pl.when(chip == row)
    def _():
        load_factor.start()

    barrier = pltpu.get_barrier_semaphore()
    peers = [(turn(row, d, rows), col) for d in range(1, rows)]
    peers += [beside(turn(chip, d, chips)) for d in range(1, chips)] + [partner]
    for device in peers:
        pl.semaphore_signal(barrier, inc=1, device_id=device, device_id_type=MESH)
    pl.semaphore_wait(barrier, len(peers))

    def scatter(op, d, source, target, device):
        return remote(source, target, scatter_send.at[op, d], scatter_recv.at[op, d], device)

    scatters = [
        (low_one, scattered.at[core]),
        (low_two, scattered_two),
        (pivot_one, scattered_pivot.at[core]),
    ]
    swapped = [scattered, scattered_pivot]
    for op, (source, target) in enumerate(scatters):
        for d in range(1, chips):
            p = turn(chip, d, chips)
            copy = scatter(op, d, source.at[0, rows_of(p)], target.at[chip], beside(p))
            copy.start()
            sent.append(copy)

    def z_line(source, direction):
        there = row + 1 if direction == UP else row - 1
        return remote(
            z.at[source, core],
            z.at[source, core],
            z_send.at[direction, source],
            z_recv.at[source],
            (there, col),
        )

    def z_near(source):
        return remote(
            z.at[source, core],
            z.at[source, core],
            near_send.at[source],
            near_recv.at[source],
            partner,
        )

    def z_near_arrival(source):
        return remote(
            z.at[source, other],
            z.at[source, other],
            near_send.at[source],
            near_recv.at[source],
            partner,
        )

    for copy in loads:
        copy.wait()

    @pl.when(row + 1 < rows)
    def _():
        z_line(row, UP).start()

    @pl.when(row > 0)
    def _():
        z_line(row, DOWN).start()

    z_near(row).start()

    def factor_piece(d, part, p):
        return remote(
            whole_factor.at[rows_of(part)],
            whole_factor.at[rows_of(part)],
            factor_send.at[0, d],
            factor_recv.at[0, d],
            beside(p),
        )

    def factor_first(d, p):
        return remote(
            factor.at[0, rows_of(p)],
            whole_factor.at[rows_of(p)],
            factor_send.at[1, d],
            factor_recv.at[1, 0],
            beside(p),
        )

    @pl.when(chip == row)
    def _():
        load_factor.wait()
        for d in range(1, chips):
            p = turn(chip, d, chips)
            factor_first(d, p).start()
            factor_piece(d, chip, p).start()

    def arrivals(op, target):
        for d in range(1, chips):
            p = turn(chip, -d, chips)
            scatter(op, d, target.at[p], target.at[p], beside(p)).wait_recv()

    def swap(op):
        return remote(
            swapped[op].at[core],
            swapped[op].at[core],
            swap_send.at[op],
            swap_recv.at[op],
            partner,
        )

    def swap_arrival(op):
        return remote(
            swapped[op].at[other],
            swapped[op].at[other],
            swap_send.at[op],
            swap_recv.at[op],
            partner,
        )

    for copy in loads_low:
        copy.wait()
    arrivals(0, scatters[0][1])
    swap(0).start()
    sent.append(swap(0))
    arrivals(1, scattered_two)
    swap_arrival(0).wait_recv()
    for plane in range(rows):
        parent = parents[plane * CORES + core]
        staged[plane] = scattered[lax.rem(parent, CORES), parent // CORES]

    def pieces_for(plane):
        return [scattered.at[core, plane], scattered_two.at[plane], staged.at[plane]]

    for e in range(1, rows):
        plane = turn(row, e, rows)
        for kind, source in enumerate(pieces_for(plane)):
            copy = remote(
                source,
                low.at[row, kind, rows_of(chip)],
                low_send.at[kind, e],
                low_recv.at[kind, e],
                (plane, col),
            )
            copy.start()
            sent.append(copy)

    def own_share(kind, d, source):
        return remote(
            source,
            low.at[row, kind, rows_of(chip)],
            share_send.at[rows + kind, d],
            share_recv.at[0, d],
            beside(turn(chip, d, chips)),
        )

    for kind, source in enumerate(pieces_for(row)):
        for d in range(1, chips):
            copy = own_share(kind, d, source)
            copy.start()
            sent.append(copy)
    low[row, LOW_ONE, rows_of(chip)] = scattered[core, row]
    low[row, LOW_TWO, rows_of(chip)] = scattered_two[row]
    low[row, LOW_PARENT, rows_of(chip)] = staged[row]

    def share(e, d, p, part):
        source = turn(row, -e, rows)
        return remote(
            low.at[source, :, rows_of(part)],
            low.at[source, :, rows_of(part)],
            share_send.at[e, d],
            share_recv.at[e, d],
            beside(p),
        )

    @pl.when(chip != row)
    def _():
        factor_first(0, chip).wait_recv()
        for d in range(1, chips):
            p = turn(chip, d, chips)

            @pl.when(p != row)
            def _():
                factor_piece(d, chip, p).start()

    for e in range(1, rows):
        source = turn(row, -e, rows)
        for kind in range(KINDS):
            target = low.at[source, kind, rows_of(chip)]
            remote(
                target, target, low_send.at[kind, e], low_recv.at[kind, e], (source, col)
            ).wait_recv()
        for d in range(1, chips):
            copy = share(e, d, turn(chip, d, chips), chip)
            copy.start()
            sent.append(copy)
    arrivals(2, scatters[2][1])
    swap(1).start()
    sent.append(swap(1))

    parent = parents[mine]

    def chosen(source, at):
        value = z[source, :, 0]
        for b in range(1, owned):
            value = jnp.where(at == b, z[source, :, b], value)
        return value.reshape(CORES * width, width)

    def step(t, carry):
        source = order(t)

        @pl.when(source != row)
        def _():
            z_line(source, UP).wait_recv()

            @pl.when(jnp.logical_and(source < row, row + 1 < rows))
            def _():
                z_line(source, UP).start()

            @pl.when(jnp.logical_and(source > row, row > 0))
            def _():
                z_line(source, DOWN).start()

            z_near(source).start()

        e = lax.rem(row - source + rows, rows)
        for d in range(1, chips):
            p = turn(chip, -d, chips)
            share_arrival = remote(
                low.at[source, :, rows_of(p)],
                low.at[source, :, rows_of(p)],
                share_send.at[0, d],
                share_recv.at[e, d],
                beside(p),
            )
            share_arrival.wait_recv()
        z_near_arrival(source).wait_recv()
        at_one = lax.rem(pattern[mine, source], owned)
        at_two = lax.rem(pattern[parent, source], owned)
        rhs = split(low[source, LOW_ONE])
        lhs = split(chosen(source, at_one))
        first = dot3(lhs, rhs)
        lhs = split(chosen(source, at_two))
        second = dot3(lhs, split(low[source, LOW_PARENT]))
        third = dot3(lhs, split(low[source, LOW_TWO]))

        @pl.when(t == 0)
        def _():
            sums[0] = first
            sums[1] = second
            sums[2] = third

        @pl.when(t > 0)
        def _():
            sums[0] += first
            sums[1] += second
            sums[2] += third

        return carry

    lax.fori_loop(0, rows, step, 0)

    def store_column(at, buffer, out):
        keep = pltpu.make_async_copy(buffer.at[core], out.at[core], column_store.at[at])
        away = remote(
            buffer.at[other], out.at[core], column_send.at[at], column_recv.at[at], partner
        )
        keep.start()
        away.start()
        return keep, away

    def reduce_scatter(kind):
        for d in range(1, chips):
            p = turn(chip, d, chips)
            copy = remote(
                partial.at[kind, rows_of(p)],
                partials.at[kind, chip],
                part_send.at[kind, d],
                part_recv.at[kind, d],
                beside(p),
            )
            copy.start()
            sent.append(copy)

    slot_one = lax.rem(pattern[mine, chip], owned)
    slot_two = lax.rem(pattern[parent, chip], owned)
    column[...] = -sums[0].reshape(CORES, width, width)
    partial[DIAG] = dot3(
        split(low[chip, LOW_ONE]), split(column[slot_one]), transposed=True
    )
    stores = [store_column(0, column, out_one)]
    reduce_scatter(DIAG)

    @pl.when(chip != row)
    def _():
        for d in range(1, chips):
            factor_piece(d, turn(chip, -d, chips), partner[1]).wait_recv()

    swap_arrival(1).wait_recv()
    whole = split(whole_factor[...])
    parent_column[...] = -sums[1].reshape(CORES, width, width)
    scaled = dot3(split(-sums[1]), whole)
    product[...] = scaled.reshape(CORES, width, width)
    column_two[...] = -(scaled + sums[2]).reshape(CORES, width, width)
    two_split = split(low[chip, LOW_TWO])
    cross = dot3(split(low[chip, LOW_PARENT]), split(product[slot_two]), transposed=True)
    cross = cross - dot3(split(parent_column[slot_two]), two_split, transposed=True)
    partial[CROSS] = cross
    pivot_rows = scattered_pivot[lax.rem(parent, CORES), parent // CORES]
    partial[CROSS, rows_of(chip)] -= dot3(split(pivot_rows), whole)
    stores.append(store_column(1, column_two, out_two))
    reduce_scatter(CROSS)
    partial[SECOND] = dot3(two_split, split(column_two[slot_two]), transposed=True) + dot3(
        whole, split(partial[CROSS]), transposed=True
    )
    reduce_scatter(SECOND)

    def line(kind, source, direction):
        there = row + 1 if direction == UP else row - 1
        return remote(
            reduced.at[source, kind],
            reduced.at[source, kind],
            line_send.at[direction, kind, source],
            line_recv.at[kind, source],
            (there, col),
        )

    def last(kind, source):
        d = lax.rem(source - chip + chips, chips)
        return remote(
            reduced.at[source, kind],
            final.at[kind, rows_of(chip)],
            last_send.at[kind, source],
            last_recv.at[kind, d],
            beside(source),
        )

    def hand_on(kind, source):
        @pl.when(source != chip)
        def _():
            last(kind, source).start()

        @pl.when(source == chip)
        def _():
            final[kind, rows_of(chip)] = reduced[source, kind]

    def pass_on(kind, source):
        @pl.when(jnp.logical_and(source <= row, row + 1 < rows))
        def _():
            line(kind, source, UP).start()

        @pl.when(jnp.logical_and(source >= row, row > 0))
        def _():
            line(kind, source, DOWN).start()

    for kind in range(KINDS):
        total = partial[kind, rows_of(chip)]
        for d in range(1, chips):
            p = turn(chip, -d, chips)
            target = partials.at[kind, p]
            remote(
                target, target, part_send.at[kind, d], part_recv.at[kind, d], beside(p)
            ).wait_recv()
            total += partials[kind, p]
        reduced[row, kind] = total
        pass_on(kind, row)
        hand_on(kind, row)

    def spread(n, carry):
        t, kind = 1 + n // KINDS, lax.rem(n, KINDS)
        source = order(t)
        line(kind, source, UP).wait_recv()
        pass_on(kind, source)
        hand_on(kind, source)
        return carry

    lax.fori_loop(0, (rows - 1) * KINDS, spread, 0)

    for copy in loads_last:
        copy.wait()

    def take(kind):
        for d in range(1, chips):
            p = turn(chip, -d, chips)
            target = final.at[kind, rows_of(p)]
            remote(
                target, target, last_send.at[kind, 0], last_recv.at[kind, d], beside(p)
            ).wait_recv()

    take(DIAG)
    out_diag[0] = pivot_own[...] - final[DIAG]
    take(CROSS)
    out_cross[0] = final[CROSS]
    take(SECOND)
    out_second[0] = pivot_second[...] - final[SECOND]

    for keep, away in stores:
        keep.wait()
        away.wait_send()
        away.wait_recv()
    for copy in sent:
        copy.wait_send()

    @pl.when(chip == row)
    def _():
        for d in range(1, chips):
            p = turn(chip, d, chips)
            factor_first(d, p).wait_send()
            factor_piece(d, chip, p).wait_send()

    @pl.when(chip != row)
    def _():
        for d in range(1, chips):
            p = turn(chip, d, chips)

            @pl.when(p != row)
            def _():
                factor_piece(d, chip, p).wait_send()

    def drain(source, carry):
        z_near(source).wait_send()

        @pl.when(jnp.logical_and(source <= row, row + 1 < rows))
        def _():
            z_line(source, UP).wait_send()
            for kind in range(KINDS):
                line(kind, source, UP).wait_send()

        @pl.when(jnp.logical_and(source >= row, row > 0))
        def _():
            z_line(source, DOWN).wait_send()
            for kind in range(KINDS):
                line(kind, source, DOWN).wait_send()

        @pl.when(source != chip)
        def _():
            for kind in range(KINDS):
                last(kind, source).wait_send()

        return carry

    lax.fori_loop(0, rows, drain, 0)


def body(
    anc_inverse,
    pattern_one,
    parents,
    low_one,
    pivot_one,
    low_two,
    second_scaled_factor,
    second_pivot_inverse,
):
    rows, cols = lax.axis_size("prow"), lax.axis_size("pcol")
    width = pivot_one.shape[1]
    chips = cols // CORES
    owned = anc_inverse.shape[1] // width
    piece = width // chips
    if rows != chips:
        raise ValueError("mesh shape")
    smem = pl.BlockSpec(memory_space=pltpu.SMEM)
    anywhere = pl.BlockSpec(memory_space=pl.ANY)
    vmem = pl.BlockSpec(memory_space=pltpu.VMEM)

    def f32(*shape):
        return jax.ShapeDtypeStruct(shape, jnp.float32)

    def buffer(*shape):
        return pltpu.VMEM(shape, jnp.float32)

    dma = pltpu.SemaphoreType.DMA
    block = (width, width)
    return tuple(
        pl.pallas_call(
            functools.partial(fused_kernel, rows, cols),
            out_shape=[
                f32(CORES, *block),
                f32(1, *block),
                f32(CORES, *block),
                f32(1, *block),
                f32(1, *block),
            ],
            in_specs=[smem, smem] + [anywhere] * 6,
            out_specs=[anywhere, vmem, anywhere, vmem, vmem],
            scratch_shapes=[
                buffer(rows, CORES, owned, *block),
                buffer(rows, KINDS, *block),
                buffer(*block),
                buffer(CORES, chips, piece, width),
                buffer(CORES, chips, piece, width),
                buffer(chips, piece, width),
                buffer(rows, piece, width),
                buffer(*block),
                buffer(*block),
                buffer(KINDS, CORES * width, width),
                buffer(CORES, *block),
                buffer(CORES, *block),
                buffer(CORES, *block),
                buffer(CORES, *block),
                buffer(KINDS, *block),
                buffer(KINDS, chips, piece, width),
                buffer(rows, KINDS, piece, width),
                buffer(KINDS, *block),
                dma((owned + 6,)),
                dma((3, chips)),
                dma((3, chips)),
                dma((2, chips)),
                dma((2, chips)),
                dma((2,)),
                dma((2,)),
                dma((KINDS, rows)),
                dma((KINDS, rows)),
                dma((rows + KINDS, chips)),
                dma((rows, chips)),
                dma((2, rows)),
                dma((rows,)),
                dma((rows,)),
                dma((rows,)),
                dma((2,)),
                dma((2,)),
                dma((2,)),
                dma((KINDS, chips)),
                dma((KINDS, chips)),
                dma((2, KINDS, rows)),
                dma((KINDS, rows)),
                dma((KINDS, rows)),
                dma((KINDS, chips)),
            ],
            compiler_params=pltpu.CompilerParams(collective_id=0, has_side_effects=True),
        )(
            pattern_one,
            parents,
            anc_inverse,
            low_one,
            pivot_one,
            low_two,
            second_scaled_factor,
            second_pivot_inverse,
        )
    )


def solution(mesh):
    placed = (
        P("pcol", "prow"),
        P(),
        P(),
        P("pcol", "prow", None),
        P("pcol", None, None),
        P("pcol", "prow", None),
        P("pcol", None, None),
        P("pcol", None, None),
    )
    return jax.shard_map(
        body,
        mesh=mesh,
        in_specs=placed,
        out_specs=(
            P("prow", "pcol", None),
            P("pcol", None, None),
            P("prow", "pcol", None),
            P("pcol", None, None),
            P("pcol", None, None),
        ),
        check_vma=False,
    )
```

```python
import functools

import jax
import jax.numpy as jnp
from jax import lax
from jax.experimental import pallas as pl
from jax.experimental.pallas import tpu as pltpu
from jax.sharding import PartitionSpec as P

MESH = pl.DeviceIdType.MESH
CORES = 2
UP, DOWN = 0, 1
LOW_ONE, LOW_TWO, LOW_PARENT = 0, 1, 2
DIAG, CROSS, SECOND = 0, 1, 2
KINDS = 3


def split(x):
    hi = x.astype(jnp.bfloat16)
    return hi, (x - hi.astype(jnp.float32)).astype(jnp.bfloat16)


def dot3(left, right, transposed=False):
    contract = (((0,), (0,)), ((), ())) if transposed else (((1,), (0,)), ((), ()))
    dot = functools.partial(
        lax.dot_general, dimension_numbers=contract, preferred_element_type=jnp.float32
    )
    return dot(left[0], right[1]) + dot(left[1], right[0]) + dot(left[0], right[0])


def fused_kernel(
    rows,
    cols,
    pattern,
    parents,
    anc,
    low_one,
    pivot_one,
    low_two,
    factor,
    pivot_two,
    out_one,
    out_diag,
    out_two,
    out_cross,
    out_second,
    z,
    low,
    whole_factor,
    scattered,
    scattered_pivot,
    scattered_two,
    staged,
    pivot_own,
    pivot_second,
    sums,
    column,
    parent_column,
    product,
    column_two,
    partial,
    partials,
    reduced,
    final,
    load_sem,
    scatter_send,
    scatter_recv,
    factor_send,
    factor_recv,
    swap_send,
    swap_recv,
    low_send,
    low_recv,
    share_send,
    share_recv,
    z_send,
    z_recv,
    near_send,
    near_recv,
    column_send,
    column_recv,
    column_store,
    part_send,
    part_recv,
    line_send,
    line_recv,
    last_send,
    last_recv,
):
    row, col = lax.axis_index("prow"), lax.axis_index("pcol")
    chips = cols // CORES
    width = factor.shape[1]
    piece = width // chips
    owned = anc.shape[1] // width
    chip, core = col // CORES, lax.rem(col, CORES)
    other = 1 - core
    mine = row * CORES + core
    partner = (row, chip * CORES + other)

    def beside(p):
        return (row, p * CORES + core)

    def turn(start, d, size):
        return lax.rem(start + d + size, size)

    def rows_of(p):
        return pl.ds(pl.multiple_of(p * piece, piece), piece)

    def remote(source, target, send, recv, device):
        return pltpu.make_async_remote_copy(
            src_ref=source,
            dst_ref=target,
            send_sem=send,
            recv_sem=recv,
            device_id=device,
            device_id_type=MESH,
        )

    def order(t):
        below, above = row, rows - 1 - row
        both = 2 * jnp.minimum(below, above)
        paired = t <= both
        distance = jnp.where(paired, (t + 1) // 2, t - both // 2)
        up = jnp.where(paired, lax.rem(t, 2) == 1, above > below)
        return jnp.where(up, row + distance, row - distance)

    sent = []

    loads = [
        pltpu.make_async_copy(
            anc.at[:, pl.ds(b * width, width)], z.at[row, core, b], load_sem.at[b]
        )
        for b in range(owned)
    ]
    loads_low = [
        pltpu.make_async_copy(
            low_one.at[0, rows_of(chip)], scattered.at[core, chip], load_sem.at[owned]
        ),
        pltpu.make_async_copy(
            low_two.at[0, rows_of(chip)], scattered_two.at[chip], load_sem.at[owned + 1]
        ),
        pltpu.make_async_copy(
            pivot_one.at[0, rows_of(chip)], scattered_pivot.at[core, chip], load_sem.at[owned + 2]
        ),
    ]
    loads_last = [
        pltpu.make_async_copy(pivot_one.at[0], pivot_own, load_sem.at[owned + 3]),
        pltpu.make_async_copy(pivot_two.at[0], pivot_second, load_sem.at[owned + 4]),
    ]
    load_factor = pltpu.make_async_copy(factor.at[0], whole_factor, load_sem.at[owned + 5])
    for copy in loads + loads_low + loads_last:
        copy.start()

    @pl.when(chip == row)
    def _():
        load_factor.start()

    barrier = pltpu.get_barrier_semaphore()
    peers = [(turn(row, d, rows), col) for d in range(1, rows)]
    peers += [beside(turn(chip, d, chips)) for d in range(1, chips)] + [partner]
    for device in peers:
        pl.semaphore_signal(barrier, inc=1, device_id=device, device_id_type=MESH)
    pl.semaphore_wait(barrier, len(peers))

    def scatter(op, d, source, target, device):
        return remote(source, target, scatter_send.at[op, d], scatter_recv.at[op, d], device)

    scatters = [
        (low_one, scattered.at[core]),
        (low_two, scattered_two),
        (pivot_one, scattered_pivot.at[core]),
    ]
    swapped = [scattered, scattered_pivot]
    for op, (source, target) in enumerate(scatters):
        for d in range(1, chips):
            p = turn(chip, d, chips)
            copy = scatter(op, d, source.at[0, rows_of(p)], target.at[chip], beside(p))
            copy.start()
            sent.append(copy)

    def z_line(source, b, direction):
        there = row + 1 if direction == UP else row - 1
        return remote(
            z.at[source, core, b],
            z.at[source, core, b],
            z_send.at[direction, source, b],
            z_recv.at[source, b],
            (there, col),
        )

    def z_near(source, b):
        return remote(
            z.at[source, core, b],
            z.at[source, core, b],
            near_send.at[source, b],
            near_recv.at[source, b],
            partner,
        )

    def z_near_arrival(source, b):
        target = z.at[source, other, b]
        return remote(target, target, near_send.at[source, b], near_recv.at[source, b], partner)

    def z_pass_on(source, b):
        @pl.when(jnp.logical_and(source <= row, row + 1 < rows))
        def _():
            z_line(source, b, UP).start()

        @pl.when(jnp.logical_and(source >= row, row > 0))
        def _():
            z_line(source, b, DOWN).start()

        z_near(source, b).start()

    def z_arrive(source, b):
        z_line(source, b, UP).wait_recv()
        z_pass_on(source, b)

    for b, copy in enumerate(loads):
        copy.wait()
        z_pass_on(row, b)

    def factor_piece(d, part, p):
        return remote(
            whole_factor.at[rows_of(part)],
            whole_factor.at[rows_of(part)],
            factor_send.at[0, d],
            factor_recv.at[0, d],
            beside(p),
        )

    def factor_first(d, p):
        return remote(
            factor.at[0, rows_of(p)],
            whole_factor.at[rows_of(p)],
            factor_send.at[1, d],
            factor_recv.at[1, 0],
            beside(p),
        )

    @pl.when(chip == row)
    def _():
        load_factor.wait()
        for d in range(1, chips):
            p = turn(chip, d, chips)
            factor_first(d, p).start()
            factor_piece(d, chip, p).start()

    def arrivals(op, target):
        for d in range(1, chips):
            p = turn(chip, -d, chips)
            scatter(op, d, target.at[p], target.at[p], beside(p)).wait_recv()

    def swap(op):
        return remote(
            swapped[op].at[core],
            swapped[op].at[core],
            swap_send.at[op],
            swap_recv.at[op],
            partner,
        )

    def swap_arrival(op):
        return remote(
            swapped[op].at[other],
            swapped[op].at[other],
            swap_send.at[op],
            swap_recv.at[op],
            partner,
        )

    for copy in loads_low:
        copy.wait()
    arrivals(0, scatters[0][1])
    swap(0).start()
    sent.append(swap(0))
    arrivals(1, scattered_two)
    swap_arrival(0).wait_recv()
    for plane in range(rows):
        parent = parents[plane * CORES + core]
        staged[plane] = scattered[lax.rem(parent, CORES), parent // CORES]

    def pieces_for(plane):
        return [scattered.at[core, plane], scattered_two.at[plane], staged.at[plane]]

    for e in range(1, rows):
        plane = turn(row, e, rows)
        for kind, source in enumerate(pieces_for(plane)):
            copy = remote(
                source,
                low.at[row, kind, rows_of(chip)],
                low_send.at[kind, e],
                low_recv.at[kind, e],
                (plane, col),
            )
            copy.start()
            sent.append(copy)

    masks = [1 << n for n in range((chips - 1).bit_length())]
    trees = [masks, masks[::-1]]
    offsets = sorted(range(1, chips), key=lambda o: o.bit_count())

    def flip(p, offset):
        for mask in masks:
            if offset & mask:
                p = p + mask - 2 * mask * lax.rem(p // mask, 2)
        return p

    def half_of(p, half):
        size = piece // 2
        return pl.ds(pl.multiple_of(p * piece + half * size, size), size)

    def share(source, offset, at, part, to, half):
        e = lax.rem(row - source + rows, rows)
        target = low.at[source, :, part]
        return remote(
            target, target, share_send.at[e, offset, at], share_recv.at[e, to, half], beside(flip(chip, offset))
        )

    def own_share(kind, source, mask):
        return remote(
            source,
            low.at[row, kind, rows_of(chip)],
            share_send.at[rows + kind, mask, 0],
            share_recv.at[0, mask, 0],
            beside(flip(chip, mask)),
        )

    def share_arrive(source):
        for offset in offsets:
            origin = flip(chip, offset)
            direct = offset in masks
            if direct:
                share(source, offset, 0, rows_of(origin), offset, 0).wait_recv()
            for half, tree in enumerate(trees):
                if not direct:
                    share(source, offset, 0, half_of(origin, half), offset, half).wait_recv()
                came = max(n for n, mask in enumerate(tree) if offset & mask)
                for mask in tree[came + 1 :]:
                    copy = share(
                        source, mask, 2 * offset + half, half_of(origin, half), offset ^ mask, half
                    )
                    copy.start()
                    sent.append(copy)

    def low_arrive(source):
        e = lax.rem(row - source + rows, rows)
        for kind in range(KINDS):
            target = low.at[source, kind, rows_of(chip)]
            remote(
                target, target, low_send.at[kind, e], low_recv.at[kind, e], (source, col)
            ).wait_recv()
        for mask in masks:
            copy = share(source, mask, 0, rows_of(chip), mask, 0)
            copy.start()
            sent.append(copy)

    for kind, source in enumerate(pieces_for(row)):
        for mask in masks:
            copy = own_share(kind, source, mask)
            copy.start()
            sent.append(copy)
    low[row, LOW_ONE, rows_of(chip)] = scattered[core, row]
    low[row, LOW_TWO, rows_of(chip)] = scattered_two[row]
    low[row, LOW_PARENT, rows_of(chip)] = staged[row]

    parent = parents[mine]

    def chosen(source, at):
        value = z[source, :, 0]
        for b in range(1, owned):
            value = jnp.where(at == b, z[source, :, b], value)
        return value.reshape(CORES * width, width)

    def add_products(source, first_time):
        for b in range(owned):
            z_near_arrival(source, b).wait_recv()
        at_one = lax.rem(pattern[mine, source], owned)
        at_two = lax.rem(pattern[parent, source], owned)
        rhs = split(low[source, LOW_ONE])
        lhs = split(chosen(source, at_one))
        first = dot3(lhs, rhs)
        lhs = split(chosen(source, at_two))
        second = dot3(lhs, split(low[source, LOW_PARENT]))
        third = dot3(lhs, split(low[source, LOW_TWO]))
        for n, value in enumerate([first, second, third]):
            sums[n] = value if first_time else sums[n] + value

    sources = [order(t) for t in range(rows)]
    inner = jnp.logical_and(row > 0, row + 1 < rows)

    @pl.when(inner)
    def _():
        for b in range(owned):
            for source in sources[1:3]:
                z_arrive(source, b)

    @pl.when(jnp.logical_not(inner))
    def _():
        for b in range(owned):
            z_arrive(sources[1], b)

    share_arrive(row)
    @pl.when(chip != row)
    def _():
        factor_first(0, chip).wait_recv()
        for d in range(1, chips):
            p = turn(chip, d, chips)

            @pl.when(p != row)
            def _():
                factor_piece(d, chip, p).start()

    arrivals(2, scatters[2][1])
    swap(1).start()
    sent.append(swap(1))
    low_arrive(sources[1])

    @pl.when(jnp.logical_not(inner))
    def _():
        for b in range(owned):
            z_arrive(sources[2], b)

    low_arrive(sources[2])
    add_products(row, True)
    for source in sources[3:]:
        low_arrive(source)

    @pl.when(inner)
    def _():
        for source in sources[3:]:
            z_arrive(source, 0)

    share_arrive(sources[1])
    share_arrive(sources[2])

    @pl.when(inner)
    def _():
        for source in sources[3:]:
            for b in range(1, owned):
                z_arrive(source, b)

    add_products(sources[1], False)
    add_products(sources[2], False)
    for source in sources[3:]:
        share_arrive(source)

        @pl.when(jnp.logical_not(inner))
        def _():
            for b in range(owned):
                z_arrive(source, b)

        add_products(source, False)

    def store_column(at, buffer, out):
        keep = pltpu.make_async_copy(buffer.at[core], out.at[core], column_store.at[at])
        away = remote(
            buffer.at[other], out.at[core], column_send.at[at], column_recv.at[at], partner
        )
        keep.start()
        away.start()
        return keep, away

    def reduce_scatter(kind):
        for d in range(1, chips):
            p = turn(chip, d, chips)
            copy = remote(
                partial.at[kind, rows_of(p)],
                partials.at[kind, chip],
                part_send.at[kind, d],
                part_recv.at[kind, d],
                beside(p),
            )
            copy.start()
            sent.append(copy)

    slot_one = lax.rem(pattern[mine, chip], owned)
    slot_two = lax.rem(pattern[parent, chip], owned)
    column[...] = -sums[0].reshape(CORES, width, width)
    partial[DIAG] = dot3(
        split(low[chip, LOW_ONE]), split(column[slot_one]), transposed=True
    )
    stores = [store_column(0, column, out_one)]
    reduce_scatter(DIAG)

    @pl.when(chip != row)
    def _():
        for d in range(1, chips):
            factor_piece(d, turn(chip, -d, chips), partner[1]).wait_recv()

    swap_arrival(1).wait_recv()
    whole = split(whole_factor[...])
    parent_column[...] = -sums[1].reshape(CORES, width, width)
    scaled = dot3(split(-sums[1]), whole)
    product[...] = scaled.reshape(CORES, width, width)
    column_two[...] = -(scaled + sums[2]).reshape(CORES, width, width)
    two_split = split(low[chip, LOW_TWO])
    cross = dot3(split(low[chip, LOW_PARENT]), split(product[slot_two]), transposed=True)
    cross = cross - dot3(split(parent_column[slot_two]), two_split, transposed=True)
    partial[CROSS] = cross
    pivot_rows = scattered_pivot[lax.rem(parent, CORES), parent // CORES]
    partial[CROSS, rows_of(chip)] -= dot3(split(pivot_rows), whole)
    stores.append(store_column(1, column_two, out_two))
    reduce_scatter(CROSS)
    partial[SECOND] = dot3(two_split, split(column_two[slot_two]), transposed=True) + dot3(
        whole, split(partial[CROSS]), transposed=True
    )
    reduce_scatter(SECOND)

    def line(kind, source, direction):
        there = row + 1 if direction == UP else row - 1
        return remote(
            reduced.at[source, kind],
            reduced.at[source, kind],
            line_send.at[direction, kind, source],
            line_recv.at[kind, source],
            (there, col),
        )

    def last(kind, source):
        d = lax.rem(source - chip + chips, chips)
        return remote(
            reduced.at[source, kind],
            final.at[kind, rows_of(chip)],
            last_send.at[kind, source],
            last_recv.at[kind, d],
            beside(source),
        )

    def hand_on(kind, source):
        @pl.when(source != chip)
        def _():
            last(kind, source).start()

        @pl.when(source == chip)
        def _():
            final[kind, rows_of(chip)] = reduced[source, kind]

    def pass_on(kind, source):
        @pl.when(jnp.logical_and(source <= row, row + 1 < rows))
        def _():
            line(kind, source, UP).start()

        @pl.when(jnp.logical_and(source >= row, row > 0))
        def _():
            line(kind, source, DOWN).start()

    for kind in range(KINDS):
        total = partial[kind, rows_of(chip)]
        for d in range(1, chips):
            p = turn(chip, -d, chips)
            target = partials.at[kind, p]
            remote(
                target, target, part_send.at[kind, d], part_recv.at[kind, d], beside(p)
            ).wait_recv()
            total += partials[kind, p]
        reduced[row, kind] = total
        pass_on(kind, row)
        hand_on(kind, row)

    def spread(n, carry):
        t, kind = 1 + n // KINDS, lax.rem(n, KINDS)
        source = order(t)
        line(kind, source, UP).wait_recv()
        pass_on(kind, source)
        hand_on(kind, source)
        return carry

    lax.fori_loop(0, (rows - 1) * KINDS, spread, 0)

    for copy in loads_last:
        copy.wait()

    def take(kind):
        for d in range(1, chips):
            p = turn(chip, -d, chips)
            target = final.at[kind, rows_of(p)]
            remote(
                target, target, last_send.at[kind, 0], last_recv.at[kind, d], beside(p)
            ).wait_recv()

    take(DIAG)
    out_diag[0] = pivot_own[...] - final[DIAG]
    take(CROSS)
    out_cross[0] = final[CROSS]
    take(SECOND)
    out_second[0] = pivot_second[...] - final[SECOND]

    for keep, away in stores:
        keep.wait()
        away.wait_send()
        away.wait_recv()
    for copy in sent:
        copy.wait_send()

    @pl.when(chip == row)
    def _():
        for d in range(1, chips):
            p = turn(chip, d, chips)
            factor_first(d, p).wait_send()
            factor_piece(d, chip, p).wait_send()

    @pl.when(chip != row)
    def _():
        for d in range(1, chips):
            p = turn(chip, d, chips)

            @pl.when(p != row)
            def _():
                factor_piece(d, chip, p).wait_send()

    def drain(source, carry):
        for b in range(owned):
            z_near(source, b).wait_send()

        @pl.when(jnp.logical_and(source <= row, row + 1 < rows))
        def _():
            for b in range(owned):
                z_line(source, b, UP).wait_send()
            for kind in range(KINDS):
                line(kind, source, UP).wait_send()

        @pl.when(jnp.logical_and(source >= row, row > 0))
        def _():
            for b in range(owned):
                z_line(source, b, DOWN).wait_send()
            for kind in range(KINDS):
                line(kind, source, DOWN).wait_send()

        @pl.when(source != chip)
        def _():
            for kind in range(KINDS):
                last(kind, source).wait_send()

        return carry

    lax.fori_loop(0, rows, drain, 0)


def body(
    anc_inverse,
    pattern_one,
    parents,
    low_one,
    pivot_one,
    low_two,
    second_scaled_factor,
    second_pivot_inverse,
):
    rows, cols = lax.axis_size("prow"), lax.axis_size("pcol")
    width = pivot_one.shape[1]
    chips = cols // CORES
    owned = anc_inverse.shape[1] // width
    piece = width // chips
    if rows != chips:
        raise ValueError("mesh shape")
    smem = pl.BlockSpec(memory_space=pltpu.SMEM)
    anywhere = pl.BlockSpec(memory_space=pl.ANY)
    vmem = pl.BlockSpec(memory_space=pltpu.VMEM)

    def f32(*shape):
        return jax.ShapeDtypeStruct(shape, jnp.float32)

    def buffer(*shape):
        return pltpu.VMEM(shape, jnp.float32)

    dma = pltpu.SemaphoreType.DMA
    block = (width, width)
    return tuple(
        pl.pallas_call(
            functools.partial(fused_kernel, rows, cols),
            out_shape=[
                f32(CORES, *block),
                f32(1, *block),
                f32(CORES, *block),
                f32(1, *block),
                f32(1, *block),
            ],
            in_specs=[smem, smem] + [anywhere] * 6,
            out_specs=[anywhere, vmem, anywhere, vmem, vmem],
            scratch_shapes=[
                buffer(rows, CORES, owned, *block),
                buffer(rows, KINDS, *block),
                buffer(*block),
                buffer(CORES, chips, piece, width),
                buffer(CORES, chips, piece, width),
                buffer(chips, piece, width),
                buffer(rows, piece, width),
                buffer(*block),
                buffer(*block),
                buffer(KINDS, CORES * width, width),
                buffer(CORES, *block),
                buffer(CORES, *block),
                buffer(CORES, *block),
                buffer(CORES, *block),
                buffer(KINDS, *block),
                buffer(KINDS, chips, piece, width),
                buffer(rows, KINDS, piece, width),
                buffer(KINDS, *block),
                dma((owned + 6,)),
                dma((3, chips)),
                dma((3, chips)),
                dma((2, chips)),
                dma((2, chips)),
                dma((2,)),
                dma((2,)),
                dma((KINDS, rows)),
                dma((KINDS, rows)),
                dma((rows + KINDS, chips, 2 * chips)),
                dma((rows, chips, 2)),
                dma((2, rows, owned)),
                dma((rows, owned)),
                dma((rows, owned)),
                dma((rows, owned)),
                dma((2,)),
                dma((2,)),
                dma((2,)),
                dma((KINDS, chips)),
                dma((KINDS, chips)),
                dma((2, KINDS, rows)),
                dma((KINDS, rows)),
                dma((KINDS, rows)),
                dma((KINDS, chips)),
            ],
            compiler_params=pltpu.CompilerParams(collective_id=0, has_side_effects=True),
        )(
            pattern_one,
            parents,
            anc_inverse,
            low_one,
            pivot_one,
            low_two,
            second_scaled_factor,
            second_pivot_inverse,
        )
    )


def solution(mesh):
    placed = (
        P("pcol", "prow"),
        P(),
        P(),
        P("pcol", "prow", None),
        P("pcol", None, None),
        P("pcol", "prow", None),
        P("pcol", None, None),
        P("pcol", None, None),
    )
    return jax.shard_map(
        body,
        mesh=mesh,
        in_specs=placed,
        out_specs=(
            P("prow", "pcol", None),
            P("pcol", None, None),
            P("prow", "pcol", None),
            P("pcol", None, None),
            P("pcol", None, None),
        ),
        check_vma=False,
    )
```

```python
import functools

import jax
import jax.numpy as jnp
from jax import lax
from jax.experimental import pallas as pl
from jax.experimental.pallas import tpu as pltpu
from jax.sharding import PartitionSpec as P

MESH = pl.DeviceIdType.MESH
CORES = 2
UP, DOWN = 0, 1
LOW_ONE, LOW_TWO, LOW_PARENT = 0, 1, 2
DIAG, CROSS, SECOND = 0, 1, 2
KINDS = 3


def split(x):
    hi = x.astype(jnp.bfloat16)
    return hi, (x - hi.astype(jnp.float32)).astype(jnp.bfloat16)


def dot3(left, right, transposed=False):
    contract = (((0,), (0,)), ((), ())) if transposed else (((1,), (0,)), ((), ()))
    dot = functools.partial(
        lax.dot_general, dimension_numbers=contract, preferred_element_type=jnp.float32
    )
    return dot(left[0], right[1]) + dot(left[1], right[0]) + dot(left[0], right[0])


def fused_kernel(
    rows,
    cols,
    pattern,
    parents,
    anc,
    low_one,
    pivot_one,
    low_two,
    factor,
    out_one,
    out_two,
    final,
    z,
    low,
    whole_factor,
    scattered,
    scattered_pivot,
    scattered_two,
    staged,
    sums,
    column,
    parent_column,
    product,
    column_two,
    partial,
    partials,
    reduced,
    load_sem,
    scatter_send,
    scatter_recv,
    factor_send,
    factor_recv,
    swap_send,
    swap_recv,
    low_send,
    low_recv,
    share_send,
    share_recv,
    z_send,
    z_recv,
    near_send,
    near_recv,
    column_send,
    column_recv,
    column_store,
    part_send,
    part_recv,
    line_send,
    line_recv,
    last_send,
    last_recv,
):
    row, col = lax.axis_index("prow"), lax.axis_index("pcol")
    chips = cols // CORES
    width = factor.shape[1]
    piece = width // chips
    owned = anc.shape[1] // width
    chip, core = col // CORES, lax.rem(col, CORES)
    other = 1 - core
    mine = row * CORES + core
    partner = (row, chip * CORES + other)

    def beside(p):
        return (row, p * CORES + core)

    def turn(start, d, size):
        return lax.rem(start + d + size, size)

    def rows_of(p):
        return pl.ds(pl.multiple_of(p * piece, piece), piece)

    def remote(source, target, send, recv, device):
        return pltpu.make_async_remote_copy(
            src_ref=source,
            dst_ref=target,
            send_sem=send,
            recv_sem=recv,
            device_id=device,
            device_id_type=MESH,
        )

    def order(t):
        below, above = row, rows - 1 - row
        both = 2 * jnp.minimum(below, above)
        paired = t <= both
        distance = jnp.where(paired, (t + 1) // 2, t - both // 2)
        up = jnp.where(paired, lax.rem(t, 2) == 1, above > below)
        return jnp.where(up, row + distance, row - distance)

    sent = []

    loads = [
        pltpu.make_async_copy(
            anc.at[:, pl.ds(b * width, width)], z.at[row, core, b], load_sem.at[b]
        )
        for b in range(owned)
    ]
    loads_low = [
        pltpu.make_async_copy(
            low_one.at[0, rows_of(chip)], scattered.at[core, chip], load_sem.at[owned]
        ),
        pltpu.make_async_copy(
            low_two.at[0, rows_of(chip)], scattered_two.at[chip], load_sem.at[owned + 1]
        ),
        pltpu.make_async_copy(
            pivot_one.at[0, rows_of(chip)], scattered_pivot.at[core, chip], load_sem.at[owned + 2]
        ),
    ]
    load_factor = pltpu.make_async_copy(factor.at[0], whole_factor, load_sem.at[owned + 3])
    for copy in loads + loads_low:
        copy.start()

    @pl.when(chip == row)
    def _():
        load_factor.start()

    barrier = pltpu.get_barrier_semaphore()
    peers = [(turn(row, d, rows), col) for d in range(1, rows)]
    peers += [beside(turn(chip, d, chips)) for d in range(1, chips)] + [partner]
    for device in peers:
        pl.semaphore_signal(barrier, inc=1, device_id=device, device_id_type=MESH)
    pl.semaphore_wait(barrier, len(peers))

    def scatter(op, d, source, target, device):
        return remote(source, target, scatter_send.at[op, d], scatter_recv.at[op, d], device)

    scatters = [
        (low_one, scattered.at[core]),
        (low_two, scattered_two),
        (pivot_one, scattered_pivot.at[core]),
    ]
    swapped = [scattered, scattered_pivot]

    def scatter_all(op):
        source, target = scatters[op]
        for d in range(1, chips):
            p = turn(chip, d, chips)
            copy = scatter(op, d, source.at[0, rows_of(p)], target.at[chip], beside(p))
            copy.start()
            sent.append(copy)

    scatter_all(0)
    scatter_all(1)

    def z_line(source, b, direction):
        there = row + 1 if direction == UP else row - 1
        return remote(
            z.at[source, core, b],
            z.at[source, core, b],
            z_send.at[direction, source, b],
            z_recv.at[source, b],
            (there, col),
        )

    def z_near(source, b):
        return remote(
            z.at[source, core, b],
            z.at[source, core, b],
            near_send.at[source, b],
            near_recv.at[source, b],
            partner,
        )

    def z_near_arrival(source, b):
        target = z.at[source, other, b]
        return remote(target, target, near_send.at[source, b], near_recv.at[source, b], partner)

    def z_pass_on(source, b):
        @pl.when(jnp.logical_and(source <= row, row + 1 < rows))
        def _():
            z_line(source, b, UP).start()

        @pl.when(jnp.logical_and(source >= row, row > 0))
        def _():
            z_line(source, b, DOWN).start()

        z_near(source, b).start()

    def z_arrive(source, b):
        z_line(source, b, UP).wait_recv()
        z_pass_on(source, b)

    for b, copy in enumerate(loads):
        copy.wait()
        z_pass_on(row, b)

    def factor_piece(d, part, p):
        return remote(
            whole_factor.at[rows_of(part)],
            whole_factor.at[rows_of(part)],
            factor_send.at[0, d],
            factor_recv.at[0, d],
            beside(p),
        )

    def factor_first(d, p):
        return remote(
            factor.at[0, rows_of(p)],
            whole_factor.at[rows_of(p)],
            factor_send.at[1, d],
            factor_recv.at[1, 0],
            beside(p),
        )

    def arrivals(op, target):
        for d in range(1, chips):
            p = turn(chip, -d, chips)
            scatter(op, d, target.at[p], target.at[p], beside(p)).wait_recv()

    def swap(op):
        return remote(
            swapped[op].at[core],
            swapped[op].at[core],
            swap_send.at[op],
            swap_recv.at[op],
            partner,
        )

    def swap_arrival(op):
        return remote(
            swapped[op].at[other],
            swapped[op].at[other],
            swap_send.at[op],
            swap_recv.at[op],
            partner,
        )

    for copy in loads_low:
        copy.wait()
    arrivals(0, scatters[0][1])
    swap(0).start()
    sent.append(swap(0))
    arrivals(1, scattered_two)
    swap_arrival(0).wait_recv()
    for plane in range(rows):
        parent = parents[plane * CORES + core]
        staged[plane] = scattered[lax.rem(parent, CORES), parent // CORES]

    def pieces_for(plane):
        return [scattered.at[core, plane], scattered_two.at[plane], staged.at[plane]]

    sources = [order(t) for t in range(rows)]
    for plane in sources[1:]:
        e = lax.rem(plane - row + rows, rows)
        for kind, source in enumerate(pieces_for(plane)):
            copy = remote(
                source,
                low.at[row, kind, rows_of(chip)],
                low_send.at[kind, e],
                low_recv.at[kind, e],
                (plane, col),
            )
            copy.start()
            sent.append(copy)

    masks = [1 << n for n in range((chips - 1).bit_length())]
    trees = [masks, masks[::-1]]
    offsets = sorted(range(1, chips), key=lambda o: o.bit_count())

    def flip(p, offset):
        for mask in masks:
            if offset & mask:
                p = p + mask - 2 * mask * lax.rem(p // mask, 2)
        return p

    def half_of(p, half):
        size = piece // 2
        return pl.ds(pl.multiple_of(p * piece + half * size, size), size)

    def share(source, offset, at, part, to, half):
        e = lax.rem(row - source + rows, rows)
        target = low.at[source, :, part]
        return remote(
            target, target, share_send.at[e, offset, at], share_recv.at[e, to, half], beside(flip(chip, offset))
        )

    def own_share(kind, source, mask):
        return remote(
            source,
            low.at[row, kind, rows_of(chip)],
            share_send.at[rows + kind, mask, 0],
            share_recv.at[0, mask, 0],
            beside(flip(chip, mask)),
        )

    def share_wait(source, offset, half):
        origin = flip(chip, offset)
        if offset not in masks:
            share(source, offset, 0, half_of(origin, half), offset, half).wait_recv()
        elif half == 0:
            share(source, offset, 0, rows_of(origin), offset, 0).wait_recv()

    def share_relay(source, last_hop):
        for offset in offsets:
            ways = [
                (half, tree[max(n for n, mask in enumerate(tree) if offset & mask) + 1 :])
                for half, tree in enumerate(trees)
            ]
            if last_hop != (not any(onward for _, onward in ways)):
                continue
            for half, onward in ways:
                share_wait(source, offset, half)
                for mask in onward:
                    copy = share(
                        source,
                        mask,
                        2 * offset + half,
                        half_of(flip(chip, offset), half),
                        offset ^ mask,
                        half,
                    )
                    copy.start()
                    sent.append(copy)

    def low_arrive(source):
        e = lax.rem(row - source + rows, rows)
        for kind in range(KINDS):
            target = low.at[source, kind, rows_of(chip)]
            remote(
                target, target, low_send.at[kind, e], low_recv.at[kind, e], (source, col)
            ).wait_recv()
        for mask in masks:
            copy = share(source, mask, 0, rows_of(chip), mask, 0)
            copy.start()
            sent.append(copy)

    for kind, source in enumerate(pieces_for(row)):
        for mask in masks:
            copy = own_share(kind, source, mask)
            copy.start()
            sent.append(copy)
    low[row, LOW_ONE, rows_of(chip)] = scattered[core, row]
    low[row, LOW_TWO, rows_of(chip)] = scattered_two[row]
    low[row, LOW_PARENT, rows_of(chip)] = staged[row]

    parent = parents[mine]

    def chosen(source, at):
        value = z[source, :, 0]
        for b in range(1, owned):
            value = jnp.where(at == b, z[source, :, b], value)
        return value.reshape(CORES * width, width)

    def add_products(source, first_time):
        for b in range(owned):
            z_near_arrival(source, b).wait_recv()
        at_one = lax.rem(pattern[mine, source], owned)
        at_two = lax.rem(pattern[parent, source], owned)
        rhs = split(low[source, LOW_ONE])
        lhs = split(chosen(source, at_one))
        first = dot3(lhs, rhs)
        lhs = split(chosen(source, at_two))
        second = dot3(lhs, split(low[source, LOW_PARENT]))
        third = dot3(lhs, split(low[source, LOW_TWO]))
        for n, value in enumerate([first, second, third]):
            sums[n] = value if first_time else sums[n] + value

    @pl.when(chip == row)
    def _():
        load_factor.wait()
        for d in range(1, chips):
            p = turn(chip, d, chips)
            factor_first(d, p).start()
            factor_piece(d, chip, p).start()

    scatter_all(2)
    inner = jnp.logical_and(row > 0, row + 1 < rows)

    @pl.when(inner)
    def _():
        for b in range(owned):
            for source in sources[1:3]:
                z_arrive(source, b)

    @pl.when(jnp.logical_not(inner))
    def _():
        for b in range(owned):
            z_arrive(sources[1], b)

    share_relay(row, False)
    low_arrive(sources[1])
    low_arrive(sources[2])
    share_relay(row, True)
    @pl.when(chip != row)
    def _():
        factor_first(0, chip).wait_recv()
        for d in range(1, chips):
            p = turn(chip, d, chips)

            @pl.when(p != row)
            def _():
                factor_piece(d, chip, p).start()

    add_products(row, True)
    share_relay(sources[1], False)
    for source in sources[3:]:
        low_arrive(source)

    @pl.when(inner)
    def _():
        for source in sources[3:]:
            z_arrive(source, 0)

    for source in sources[2:]:
        share_relay(source, False)

    @pl.when(inner)
    def _():
        for source in sources[3:]:
            for b in range(1, owned):
                z_arrive(source, b)

    share_relay(sources[1], True)
    add_products(sources[1], False)
    arrivals(2, scatters[2][1])
    swap(1).start()
    sent.append(swap(1))
    for source in sources[2:]:
        share_relay(source, True)

        @pl.when(jnp.logical_not(inner))
        def _():
            for b in range(owned):
                z_arrive(source, b)

        add_products(source, False)

    def store_column(at, buffer, out):
        keep = pltpu.make_async_copy(buffer.at[core], out.at[core], column_store.at[at])
        away = remote(
            buffer.at[other], out.at[core], column_send.at[at], column_recv.at[at], partner
        )
        keep.start()
        away.start()
        return keep, away

    def reduce_scatter(kind):
        for d in range(1, chips):
            p = turn(chip, d, chips)
            copy = remote(
                partial.at[kind, rows_of(p)],
                partials.at[kind, chip],
                part_send.at[kind, d],
                part_recv.at[kind, d],
                beside(p),
            )
            copy.start()
            sent.append(copy)

    slot_one = lax.rem(pattern[mine, chip], owned)
    slot_two = lax.rem(pattern[parent, chip], owned)
    column[...] = -sums[0].reshape(CORES, width, width)
    partial[DIAG] = dot3(
        split(low[chip, LOW_ONE]), split(column[slot_one]), transposed=True
    )
    stores = [store_column(0, column, out_one)]
    reduce_scatter(DIAG)

    @pl.when(chip != row)
    def _():
        for d in range(1, chips):
            factor_piece(d, turn(chip, -d, chips), partner[1]).wait_recv()

    swap_arrival(1).wait_recv()
    whole = split(whole_factor[...])
    parent_column[...] = -sums[1].reshape(CORES, width, width)
    scaled = dot3(split(-sums[1]), whole)
    product[...] = scaled.reshape(CORES, width, width)
    column_two[...] = -(scaled + sums[2]).reshape(CORES, width, width)
    two_split = split(low[chip, LOW_TWO])
    cross = dot3(split(low[chip, LOW_PARENT]), split(product[slot_two]), transposed=True)
    cross = cross - dot3(split(parent_column[slot_two]), two_split, transposed=True)
    partial[CROSS] = cross
    pivot_rows = scattered_pivot[lax.rem(parent, CORES), parent // CORES]
    partial[CROSS, rows_of(chip)] -= dot3(split(pivot_rows), whole)
    stores.append(store_column(1, column_two, out_two))
    reduce_scatter(CROSS)
    partial[SECOND] = dot3(two_split, split(column_two[slot_two]), transposed=True) + dot3(
        whole, split(partial[CROSS]), transposed=True
    )
    reduce_scatter(SECOND)

    def line(kind, source, distance):
        way = UP if distance > 0 else DOWN
        return remote(
            reduced.at[source, kind],
            reduced.at[source, kind],
            line_send.at[way, kind, source, abs(distance) // 2],
            line_recv.at[kind, source],
            (row + distance, col),
        )

    def onward(source, act):
        for distance in range(1, rows, 2):

            @pl.when(jnp.logical_and(source == row, row + distance < rows))
            def _():
                act(distance)

            @pl.when(jnp.logical_and(source == row, row >= distance))
            def _():
                act(-distance)

        @pl.when(jnp.logical_and(lax.rem(row - source + 2 * rows, 2) == 1, source < row))
        def _():
            @pl.when(row + 1 < rows)
            def _():
                act(1)

        @pl.when(jnp.logical_and(lax.rem(row - source + 2 * rows, 2) == 1, source > row))
        def _():
            @pl.when(row > 0)
            def _():
                act(-1)

    def last(kind, source):
        d = lax.rem(source - chip + chips, chips)
        return remote(
            reduced.at[source, kind],
            final.at[kind, rows_of(chip)],
            last_send.at[kind, source],
            last_recv.at[kind, d],
            beside(source),
        )

    def hand_on(kind, source):
        @pl.when(source != chip)
        def _():
            last(kind, source).start()

        @pl.when(source == chip)
        def _():
            final[kind, rows_of(chip)] = reduced[source, kind]

    def pass_on(kind, source):
        onward(source, lambda distance: line(kind, source, distance).start())

    for kind in range(KINDS):
        total = partial[kind, rows_of(chip)]
        for d in range(1, chips):
            p = turn(chip, -d, chips)
            target = partials.at[kind, p]
            remote(
                target, target, part_send.at[kind, d], part_recv.at[kind, d], beside(p)
            ).wait_recv()
            total += partials[kind, p]
        reduced[row, kind] = total
        pass_on(kind, row)
        hand_on(kind, row)

    def spread(kind, source):
        @pl.when(source != row)
        def _():
            line(kind, source, 1).wait_recv()
            pass_on(kind, source)
            hand_on(kind, source)

    for source in range(1, rows - 1):
        for kind in range(KINDS):
            spread(kind, source)
    near_end = jnp.where(2 * row < rows, 0, rows - 1)
    spread(0, near_end)
    for kind in range(1, KINDS):
        spread(kind, near_end)
        spread(kind - 1, rows - 1 - near_end)
    spread(KINDS - 1, rows - 1 - near_end)

    def take(kind):
        for d in range(1, chips):
            p = turn(chip, -d, chips)
            target = final.at[kind, rows_of(p)]
            remote(
                target, target, last_send.at[kind, 0], last_recv.at[kind, d], beside(p)
            ).wait_recv()

    for kind in range(KINDS):
        take(kind)

    for keep, away in stores:
        keep.wait()
        away.wait_send()
        away.wait_recv()
    for copy in sent:
        copy.wait_send()

    @pl.when(chip == row)
    def _():
        for d in range(1, chips):
            p = turn(chip, d, chips)
            factor_first(d, p).wait_send()
            factor_piece(d, chip, p).wait_send()

    @pl.when(chip != row)
    def _():
        for d in range(1, chips):
            p = turn(chip, d, chips)

            @pl.when(p != row)
            def _():
                factor_piece(d, chip, p).wait_send()

    def drain(source, carry):
        for b in range(owned):
            z_near(source, b).wait_send()
        @pl.when(jnp.logical_and(source <= row, row + 1 < rows))
        def _():
            for b in range(owned):
                z_line(source, b, UP).wait_send()

        @pl.when(jnp.logical_and(source >= row, row > 0))
        def _():
            for b in range(owned):
                z_line(source, b, DOWN).wait_send()

        for kind in range(KINDS):
            onward(source, lambda distance: line(kind, source, distance).wait_send())

        @pl.when(source != chip)
        def _():
            for kind in range(KINDS):
                last(kind, source).wait_send()

        return carry

    lax.fori_loop(0, rows, drain, 0)


def finish_kernel(
    column_one, column_two, final, pivot_one, pivot_two, out_one, out_diag, out_two, out_cross, out_second
):
    out_one[...] = column_one[...]
    out_diag[0] = pivot_one[0] - final[DIAG]
    out_two[...] = column_two[...]
    out_cross[0] = final[CROSS]
    out_second[0] = pivot_two[0] - final[SECOND]


def body(
    anc_inverse,
    pattern_one,
    parents,
    low_one,
    pivot_one,
    low_two,
    second_scaled_factor,
    second_pivot_inverse,
):
    rows, cols = lax.axis_size("prow"), lax.axis_size("pcol")
    width = pivot_one.shape[1]
    chips = cols // CORES
    owned = anc_inverse.shape[1] // width
    piece = width // chips
    if rows != chips:
        raise ValueError("mesh shape")
    smem = pl.BlockSpec(memory_space=pltpu.SMEM)
    anywhere = pl.BlockSpec(memory_space=pl.ANY)
    vmem = pl.BlockSpec(memory_space=pltpu.VMEM)

    def f32(*shape):
        return jax.ShapeDtypeStruct(shape, jnp.float32)

    def buffer(*shape):
        return pltpu.VMEM(shape, jnp.float32)

    dma = pltpu.SemaphoreType.DMA
    block = (width, width)
    column_one, column_two, final = pl.pallas_call(
        functools.partial(fused_kernel, rows, cols),
        out_shape=[f32(CORES, *block), f32(CORES, *block), f32(KINDS, *block)],
        in_specs=[smem, smem] + [anywhere] * 5,
        out_specs=[anywhere, anywhere, vmem],
        scratch_shapes=[
            buffer(rows, CORES, owned, *block),
            buffer(rows, KINDS, *block),
            buffer(*block),
            buffer(CORES, chips, piece, width),
            buffer(CORES, chips, piece, width),
            buffer(chips, piece, width),
            buffer(rows, piece, width),
            buffer(KINDS, CORES * width, width),
            buffer(CORES, *block),
            buffer(CORES, *block),
            buffer(CORES, *block),
            buffer(CORES, *block),
            buffer(KINDS, *block),
            buffer(KINDS, chips, piece, width),
            buffer(rows, KINDS, piece, width),
            dma((owned + 4,)),
            dma((3, chips)),
            dma((3, chips)),
            dma((2, chips)),
            dma((2, chips)),
            dma((2,)),
            dma((2,)),
            dma((KINDS, rows)),
            dma((KINDS, rows)),
            dma((rows + KINDS, chips, 2 * chips)),
            dma((rows, chips, 2)),
            dma((2, rows, owned)),
            dma((rows, owned)),
            dma((rows, owned)),
            dma((rows, owned)),
            dma((2,)),
            dma((2,)),
            dma((2,)),
            dma((KINDS, chips)),
            dma((KINDS, chips)),
            dma((2, KINDS, rows, rows)),
            dma((KINDS, rows)),
            dma((KINDS, rows)),
            dma((KINDS, chips)),
        ],
        compiler_params=pltpu.CompilerParams(collective_id=0, has_side_effects=True),
    )(pattern_one, parents, anc_inverse, low_one, pivot_one, low_two, second_scaled_factor)
    return tuple(
        pl.pallas_call(
            finish_kernel,
            out_shape=[
                f32(CORES, *block),
                f32(1, *block),
                f32(CORES, *block),
                f32(1, *block),
                f32(1, *block),
            ],
            in_specs=[vmem] * 5,
            out_specs=[vmem] * 5,
        )(column_one, column_two, final, pivot_one, second_pivot_inverse)
    )


def solution(mesh):
    placed = (
        P("pcol", "prow"),
        P(),
        P(),
        P("pcol", "prow", None),
        P("pcol", None, None),
        P("pcol", "prow", None),
        P("pcol", None, None),
        P("pcol", None, None),
    )
    return jax.shard_map(
        body,
        mesh=mesh,
        in_specs=placed,
        out_specs=(
            P("prow", "pcol", None),
            P("pcol", None, None),
            P("prow", "pcol", None),
            P("pcol", None, None),
            P("pcol", None, None),
        ),
        check_vma=False,
    )
```

```python
import functools

import jax
import jax.numpy as jnp
from jax import lax
from jax.experimental import pallas as pl
from jax.experimental.pallas import tpu as pltpu
from jax.sharding import PartitionSpec as P

MESH = pl.DeviceIdType.MESH
CORES = 2
UP, DOWN = 0, 1
LOW_ONE, LOW_TWO, LOW_PARENT = 0, 1, 2
DIAG, CROSS, SECOND = 0, 1, 2
KINDS = 3
PARTS = 1
STRIPS = [(kind, part) for kind in range(KINDS) for part in range(PARTS)]


def split(x):
    hi = x.astype(jnp.bfloat16)
    return hi, (x - hi.astype(jnp.float32)).astype(jnp.bfloat16)


def dot3(left, right, transposed=False):
    contract = (((0,), (0,)), ((), ())) if transposed else (((1,), (0,)), ((), ()))
    dot = functools.partial(
        lax.dot_general, dimension_numbers=contract, preferred_element_type=jnp.float32
    )
    return dot(left[0], right[1]) + dot(left[1], right[0]) + dot(left[0], right[0])


def fused_kernel(
    rows,
    cols,
    pattern_table,
    parents_table,
    anc,
    low_one,
    pivot_one,
    low_two,
    factor,
    out_one,
    out_two,
    final,
    pattern,
    parents,
    z,
    low,
    whole_factor,
    scattered,
    scattered_pivot,
    scattered_two,
    staged,
    sums,
    column,
    parent_column,
    product,
    column_two,
    partial,
    partials,
    reduced,
    load_sem,
    scatter_send,
    scatter_recv,
    factor_send,
    factor_recv,
    swap_send,
    swap_recv,
    low_send,
    low_recv,
    share_send,
    share_recv,
    z_send,
    z_recv,
    near_send,
    near_recv,
    column_send,
    column_recv,
    column_store,
    part_send,
    part_recv,
    line_send,
    line_recv,
    last_send,
    last_recv,
):
    row, col = lax.axis_index("prow"), lax.axis_index("pcol")
    chips = cols // CORES
    width = factor.shape[1]
    piece = width // chips
    owned = anc.shape[1] // width
    chip, core = col // CORES, lax.rem(col, CORES)
    other = 1 - core
    mine = row * CORES + core
    partner = (row, chip * CORES + other)

    def beside(p):
        return (row, p * CORES + core)

    def turn(start, d, size):
        return lax.rem(start + d + size, size)

    def rows_of(p):
        return pl.ds(pl.multiple_of(p * piece, piece), piece)

    strip = piece // PARTS

    def strip_of(p, part):
        return pl.ds(pl.multiple_of(p * piece + part * strip, strip), strip)

    def remote(source, target, send, recv, device):
        return pltpu.make_async_remote_copy(
            src_ref=source,
            dst_ref=target,
            send_sem=send,
            recv_sem=recv,
            device_id=device,
            device_id_type=MESH,
        )

    def order(t):
        below, above = row, rows - 1 - row
        both = 2 * jnp.minimum(below, above)
        paired = t <= both
        distance = jnp.where(paired, (t + 1) // 2, t - both // 2)
        up = jnp.where(paired, lax.rem(t, 2) == 1, above > below)
        return jnp.where(up, row + distance, row - distance)

    sent = []

    loads = [
        pltpu.make_async_copy(
            anc.at[:, pl.ds(b * width, width)], z.at[row, core, b], load_sem.at[b]
        )
        for b in range(owned)
    ]
    loads_low = [
        pltpu.make_async_copy(
            low_one.at[0, rows_of(chip)], scattered.at[core, chip], load_sem.at[owned]
        ),
        pltpu.make_async_copy(
            low_two.at[0, rows_of(chip)], scattered_two.at[chip], load_sem.at[owned + 1]
        ),
        pltpu.make_async_copy(
            pivot_one.at[0, rows_of(chip)], scattered_pivot.at[core, chip], load_sem.at[owned + 2]
        ),
    ]
    load_factor = pltpu.make_async_copy(factor.at[0], whole_factor, load_sem.at[owned + 3])
    loads_index = [
        pltpu.make_async_copy(pattern_table, pattern, load_sem.at[owned + 4]),
        pltpu.make_async_copy(parents_table, parents, load_sem.at[owned + 5]),
    ]
    for copy in loads_index + loads + loads_low:
        copy.start()

    @pl.when(chip == row)
    def _():
        load_factor.start()

    barrier = pltpu.get_barrier_semaphore()
    peers = [(turn(row, d, rows), col) for d in range(1, rows)]
    peers += [beside(turn(chip, d, chips)) for d in range(1, chips)] + [partner]
    for device in peers:
        pl.semaphore_signal(barrier, inc=1, device_id=device, device_id_type=MESH)
    pl.semaphore_wait(barrier, len(peers))

    def scatter(op, d, source, target, device):
        return remote(source, target, scatter_send.at[op, d], scatter_recv.at[op, d], device)

    scatters = [
        (low_one, scattered.at[core]),
        (low_two, scattered_two),
        (pivot_one, scattered_pivot.at[core]),
    ]
    swapped = [scattered, scattered_pivot]

    def scatter_all(op):
        source, target = scatters[op]
        for d in range(1, chips):
            p = turn(chip, d, chips)
            copy = scatter(op, d, source.at[0, rows_of(p)], target.at[chip], beside(p))
            copy.start()
            sent.append(copy)


    def z_line(source, b, direction):
        there = row + 1 if direction == UP else row - 1
        return remote(
            z.at[source, core, b],
            z.at[source, core, b],
            z_send.at[direction, source, b],
            z_recv.at[source, b],
            (there, col),
        )

    def z_near(source, b):
        return remote(
            z.at[source, core, b],
            z.at[source, core, b],
            near_send.at[source, b],
            near_recv.at[source, b],
            partner,
        )

    def z_near_arrival(source, b):
        target = z.at[source, other, b]
        return remote(target, target, near_send.at[source, b], near_recv.at[source, b], partner)

    def z_pass_on(source, b):
        @pl.when(jnp.logical_and(source <= row, row + 1 < rows))
        def _():
            z_line(source, b, UP).start()

        @pl.when(jnp.logical_and(source >= row, row > 0))
        def _():
            z_line(source, b, DOWN).start()

    def z_arrive(source, b):
        z_line(source, b, UP).wait_recv()
        z_pass_on(source, b)
        z_near(source, b).start()

    for b, copy in enumerate(loads):
        copy.wait()
        z_pass_on(row, b)

    scatter_all(0)
    scatter_all(1)
    for b in range(owned):
        z_near(row, b).start()

    def factor_piece(d, part, p):
        return remote(
            whole_factor.at[rows_of(part)],
            whole_factor.at[rows_of(part)],
            factor_send.at[0, d],
            factor_recv.at[0, d],
            beside(p),
        )

    def factor_first(d, p):
        return remote(
            factor.at[0, rows_of(p)],
            whole_factor.at[rows_of(p)],
            factor_send.at[1, d],
            factor_recv.at[1, 0],
            beside(p),
        )

    def arrivals(op, target):
        for d in range(1, chips):
            p = turn(chip, -d, chips)
            scatter(op, d, target.at[p], target.at[p], beside(p)).wait_recv()

    def swap(op):
        return remote(
            swapped[op].at[core],
            swapped[op].at[core],
            swap_send.at[op],
            swap_recv.at[op],
            partner,
        )

    def swap_arrival(op):
        return remote(
            swapped[op].at[other],
            swapped[op].at[other],
            swap_send.at[op],
            swap_recv.at[op],
            partner,
        )

    for copy in loads_low + loads_index:
        copy.wait()
    arrivals(0, scatters[0][1])
    swap(0).start()
    sent.append(swap(0))
    arrivals(1, scattered_two)
    swap_arrival(0).wait_recv()
    for plane in range(rows):
        parent = parents[plane * CORES + core]
        staged[plane] = scattered[lax.rem(parent, CORES), parent // CORES]

    def pieces_for(plane):
        return [scattered.at[core, plane], scattered_two.at[plane], staged.at[plane]]

    sources = [order(t) for t in range(rows)]
    for plane in sources[1:]:
        e = lax.rem(plane - row + rows, rows)
        for kind, source in enumerate(pieces_for(plane)):
            copy = remote(
                source,
                low.at[row, kind, rows_of(chip)],
                low_send.at[kind, e],
                low_recv.at[kind, e],
                (plane, col),
            )
            copy.start()
            sent.append(copy)

    masks = [1 << n for n in range((chips - 1).bit_length())]
    trees = [masks, masks[::-1]]
    offsets = sorted(range(1, chips), key=lambda o: o.bit_count())

    def flip(p, offset):
        for mask in masks:
            if offset & mask:
                p = p + mask - 2 * mask * lax.rem(p // mask, 2)
        return p

    def half_of(p, half):
        size = piece // 2
        return pl.ds(pl.multiple_of(p * piece + half * size, size), size)

    def share(source, offset, at, part, to, half):
        e = lax.rem(row - source + rows, rows)
        target = low.at[source, :, part]
        return remote(
            target, target, share_send.at[e, offset, at], share_recv.at[e, to, half], beside(flip(chip, offset))
        )

    def own_share(kind, source, mask):
        return remote(
            source,
            low.at[row, kind, rows_of(chip)],
            share_send.at[rows + kind, mask, 0],
            share_recv.at[0, mask, 0],
            beside(flip(chip, mask)),
        )

    def share_wait(source, offset, half):
        origin = flip(chip, offset)
        if offset not in masks:
            share(source, offset, 0, half_of(origin, half), offset, half).wait_recv()
        elif half == 0:
            share(source, offset, 0, rows_of(origin), offset, 0).wait_recv()

    def share_relay(source, last_hop):
        for offset in offsets:
            ways = [
                (half, tree[max(n for n, mask in enumerate(tree) if offset & mask) + 1 :])
                for half, tree in enumerate(trees)
            ]
            if last_hop != (not any(onward for _, onward in ways)):
                continue
            for half, onward in ways:
                share_wait(source, offset, half)
                for mask in onward:
                    copy = share(
                        source,
                        mask,
                        2 * offset + half,
                        half_of(flip(chip, offset), half),
                        offset ^ mask,
                        half,
                    )
                    copy.start()
                    sent.append(copy)

    def low_arrive(source):
        e = lax.rem(row - source + rows, rows)
        for kind in range(KINDS):
            target = low.at[source, kind, rows_of(chip)]
            remote(
                target, target, low_send.at[kind, e], low_recv.at[kind, e], (source, col)
            ).wait_recv()
        for mask in masks:
            copy = share(source, mask, 0, rows_of(chip), mask, 0)
            copy.start()
            sent.append(copy)

    for kind, source in enumerate(pieces_for(row)):
        for mask in masks:
            copy = own_share(kind, source, mask)
            copy.start()
            sent.append(copy)
    low[row, LOW_ONE, rows_of(chip)] = scattered[core, row]
    low[row, LOW_TWO, rows_of(chip)] = scattered_two[row]
    low[row, LOW_PARENT, rows_of(chip)] = staged[row]

    parent = parents[mine]

    def chosen(source, at):
        value = z[source, :, 0]
        for b in range(1, owned):
            value = jnp.where(at == b, z[source, :, b], value)
        return value.reshape(CORES * width, width)

    def store_column(at, buffer, out):
        keep = pltpu.make_async_copy(buffer.at[core], out.at[core], column_store.at[at])
        away = remote(
            buffer.at[other], out.at[core], column_send.at[at], column_recv.at[at], partner
        )
        keep.start()
        away.start()
        return keep, away

    def part_copy(kind, part, d, p, source, target):
        n = kind * PARTS + part
        return remote(source, target, part_send.at[n, d], part_recv.at[n, d], beside(p))

    def reduce_scatter(kind):
        for part in range(PARTS):
            for d in range(1, chips):
                p = turn(chip, d, chips)
                target = partials.at[kind, chip, strip_of(0, part)]
                copy = part_copy(kind, part, d, p, partial.at[kind, strip_of(p, part)], target)
                copy.start()
                sent.append(copy)

    slot_one = lax.rem(pattern[chip, mine], owned)
    slot_two = lax.rem(pattern[chip, parent], owned)
    stores = []

    def add_products(source, first_time=False, last_time=False):
        for b in range(owned):
            z_near_arrival(source, b).wait_recv()
        lhs = split(chosen(source, lax.rem(pattern[source, mine], owned)))
        first = dot3(lhs, split(low[source, LOW_ONE]))
        sums[0] = first if first_time else sums[0] + first
        if last_time:
            column[...] = -sums[0].reshape(CORES, width, width)
            partial[DIAG] = dot3(
                split(low[chip, LOW_ONE]), split(column[slot_one]), transposed=True
            )
            reduce_scatter(DIAG)
            stores.append(store_column(0, column, out_one))
        lhs = split(chosen(source, lax.rem(pattern[source, parent], owned)))
        second = dot3(lhs, split(low[source, LOW_PARENT]))
        third = dot3(lhs, split(low[source, LOW_TWO]))
        for n, value in enumerate([second, third], 1):
            sums[n] = value if first_time else sums[n] + value

    @pl.when(chip == row)
    def _():
        load_factor.wait()
        for d in range(1, chips):
            p = turn(chip, d, chips)
            factor_first(d, p).start()
            factor_piece(d, chip, p).start()

    scatter_all(2)
    inner = jnp.logical_and(row > 0, row + 1 < rows)

    @pl.when(inner)
    def _():
        for b in range(owned):
            for source in sources[1:3]:
                z_arrive(source, b)

    @pl.when(jnp.logical_not(inner))
    def _():
        for b in range(owned):
            z_arrive(sources[1], b)

    share_relay(row, False)
    low_arrive(sources[1])
    low_arrive(sources[2])
    share_relay(sources[1], False)
    for source in sources[3:]:
        low_arrive(source)
    @pl.when(inner)
    def _():
        for source in sources[3:]:
            z_arrive(source, 0)

    for source in sources[2:]:
        share_relay(source, False)

    @pl.when(inner)
    def _():
        for source in sources[3:]:
            for b in range(1, owned):
                z_arrive(source, b)

    @pl.when(chip != row)
    def _():
        factor_first(0, chip).wait_recv()
        for d in range(1, chips):
            p = turn(chip, d, chips)

            @pl.when(p != row)
            def _():
                factor_piece(d, chip, p).start()

    share_relay(row, True)
    add_products(row, True)
    share_relay(sources[1], True)
    add_products(sources[1])
    arrivals(2, scatters[2][1])
    swap(1).start()
    sent.append(swap(1))
    for source in sources[2:]:
        share_relay(source, True)

        @pl.when(jnp.logical_not(inner))
        def _():
            for b in range(owned):
                z_arrive(source, b)

        add_products(source, last_time=source is sources[-1])

    @pl.when(chip != row)
    def _():
        for d in range(1, chips):
            factor_piece(d, turn(chip, -d, chips), partner[1]).wait_recv()


    swap_arrival(1).wait_recv()
    whole = split(whole_factor[...])
    parent_column[...] = -sums[1].reshape(CORES, width, width)
    scaled = dot3(split(-sums[1]), whole)
    product[...] = scaled.reshape(CORES, width, width)
    column_two[...] = -(scaled + sums[2]).reshape(CORES, width, width)
    two_split = split(low[chip, LOW_TWO])
    cross = dot3(split(low[chip, LOW_PARENT]), split(product[slot_two]), transposed=True)
    cross = cross - dot3(split(parent_column[slot_two]), two_split, transposed=True)
    partial[CROSS] = cross
    pivot_rows = scattered_pivot[lax.rem(parent, CORES), parent // CORES]
    partial[CROSS, rows_of(chip)] -= dot3(split(pivot_rows), whole)
    stores.append(store_column(1, column_two, out_two))
    reduce_scatter(CROSS)
    partial[SECOND] = dot3(two_split, split(column_two[slot_two]), transposed=True) + dot3(
        whole, split(partial[CROSS]), transposed=True
    )
    reduce_scatter(SECOND)

    def line(kind, part, source, distance):
        way = UP if distance > 0 else DOWN
        n = kind * PARTS + part
        block = reduced.at[source, kind, strip_of(0, part)]
        return remote(
            block,
            block,
            line_send.at[way, n, source, abs(distance) - 1],
            line_recv.at[n, source],
            (row + distance, col),
        )

    def own_onward(kind, act):
        for distance in range(1, rows, 1 if kind == SECOND else 2)[::-1]:

            @pl.when(row + distance < rows)
            def _():
                act(distance)

            @pl.when(row >= distance)
            def _():
                act(-distance)

    def relay_onward(kind, source, act):
        if kind == SECOND:
            return
        odd = lax.rem(row + source, 2) == 1

        @pl.when(jnp.logical_and(odd, jnp.logical_and(source < row, row + 1 < rows)))
        def _():
            act(1)

        @pl.when(jnp.logical_and(odd, jnp.logical_and(source > row, row > 0)))
        def _():
            act(-1)

    def last(kind, part, source):
        n = kind * PARTS + part
        d = lax.rem(source - chip + chips, chips)
        return remote(
            reduced.at[source, kind, strip_of(0, part)],
            final.at[kind, strip_of(chip, part)],
            last_send.at[n, source],
            last_recv.at[n, d],
            beside(source),
        )

    def hand_on(kind, part, source):
        @pl.when(source != chip)
        def _():
            last(kind, part, source).start()

        @pl.when(source == chip)
        def _():
            final[kind, strip_of(chip, part)] = reduced[source, kind, strip_of(0, part)]

    for kind, part in STRIPS:
        total = partial[kind, strip_of(chip, part)]
        for d in range(1, chips):
            p = turn(chip, -d, chips)
            target = partials.at[kind, p, strip_of(0, part)]
            part_copy(kind, part, d, p, target, target).wait_recv()
            total += partials[kind, p, strip_of(0, part)]
        reduced[row, kind, strip_of(0, part)] = total
        own_onward(kind, lambda distance: line(kind, part, row, distance).start())
        hand_on(kind, part, row)

    def spread(kind, part, source):
        @pl.when(source != row)
        def _():
            line(kind, part, source, 1).wait_recv()
            relay_onward(
                kind, source, lambda distance: line(kind, part, source, distance).start()
            )
            hand_on(kind, part, source)

    for source in range(1, rows - 1):
        for kind, part in STRIPS:
            spread(kind, part, source)
    near_end = jnp.where(2 * row < rows, 0, rows - 1)
    lag = PARTS
    for n in range(len(STRIPS) + lag):
        if n < len(STRIPS):
            spread(*STRIPS[n], near_end)
        if n >= lag:
            spread(*STRIPS[n - lag], rows - 1 - near_end)

    for keep, away in stores:
        keep.wait()
        away.wait_send()
        away.wait_recv()
    for copy in sent:
        copy.wait_send()

    @pl.when(chip == row)
    def _():
        for d in range(1, chips):
            p = turn(chip, d, chips)
            factor_first(d, p).wait_send()
            factor_piece(d, chip, p).wait_send()

    @pl.when(chip != row)
    def _():
        for d in range(1, chips):
            p = turn(chip, d, chips)

            @pl.when(p != row)
            def _():
                factor_piece(d, chip, p).wait_send()

    def drain(source, carry):
        for b in range(owned):
            z_near(source, b).wait_send()
        @pl.when(jnp.logical_and(source <= row, row + 1 < rows))
        def _():
            for b in range(owned):
                z_line(source, b, UP).wait_send()

        @pl.when(jnp.logical_and(source >= row, row > 0))
        def _():
            for b in range(owned):
                z_line(source, b, DOWN).wait_send()

        for kind, part in STRIPS:
            relay_onward(
                kind, source, lambda distance: line(kind, part, source, distance).wait_send()
            )

        @pl.when(source != chip)
        def _():
            for kind, part in STRIPS:
                last(kind, part, source).wait_send()

        return carry

    lax.fori_loop(0, rows, drain, 0)
    for kind, part in STRIPS:
        own_onward(kind, lambda distance: line(kind, part, row, distance).wait_send())

    for kind, part in STRIPS:
        for d in range(1, chips):
            p = turn(chip, -d, chips)
            target = final.at[kind, strip_of(p, part)]
            n = kind * PARTS + part
            remote(
                target, target, last_send.at[n, 0], last_recv.at[n, d], beside(p)
            ).wait_recv()


def finish_kernel(
    column_one,
    column_two,
    final,
    pivot_one,
    pivot_two,
    out_one,
    out_diag,
    out_two,
    out_cross,
    out_second,
    one,
    two,
    sums,
    diag,
    second,
    load_sem,
    store_sem,
):
    sources = [column_one, column_two, final.at[CROSS], pivot_one.at[0], final.at[DIAG]]
    sources += [pivot_two.at[0], final.at[SECOND]]
    places = [one, two, sums.at[CROSS], diag, sums.at[DIAG], second, sums.at[SECOND]]
    loads = [
        pltpu.make_async_copy(source, place, load_sem.at[n])
        for n, (source, place) in enumerate(zip(sources, places))
    ]
    kept = [(one, out_one), (two, out_two), (sums.at[CROSS], out_cross.at[0])]
    kept += [(diag, out_diag.at[0]), (second, out_second.at[0])]
    stores = [
        pltpu.make_async_copy(place, out, store_sem.at[n]) for n, (place, out) in enumerate(kept)
    ]
    for copy in loads:
        copy.start()
    for n in range(3):
        loads[n].wait()
        stores[n].start()
    loads[3].wait()
    loads[4].wait()
    diag[...] = diag[...] - sums[DIAG]
    stores[3].start()
    loads[5].wait()
    loads[6].wait()
    second[...] = second[...] - sums[SECOND]
    stores[4].start()
    for copy in stores:
        copy.wait()


def body(
    anc_inverse,
    pattern_one,
    parents,
    low_one,
    pivot_one,
    low_two,
    second_scaled_factor,
    second_pivot_inverse,
):
    rows, cols = lax.axis_size("prow"), lax.axis_size("pcol")
    width = pivot_one.shape[1]
    chips = cols // CORES
    owned = anc_inverse.shape[1] // width
    piece = width // chips
    if rows != chips:
        raise ValueError("mesh shape")
    anywhere = pl.BlockSpec(memory_space=pl.ANY)
    vmem = pl.BlockSpec(memory_space=pltpu.VMEM)

    def f32(*shape):
        return jax.ShapeDtypeStruct(shape, jnp.float32)

    def buffer(*shape):
        return pltpu.VMEM(shape, jnp.float32)

    dma = pltpu.SemaphoreType.DMA
    block = (width, width)
    column_one, column_two, final = pl.pallas_call(
        functools.partial(fused_kernel, rows, cols),
        out_shape=[f32(CORES, *block), f32(CORES, *block), f32(KINDS, *block)],
        in_specs=[anywhere] * 7,
        out_specs=[anywhere, anywhere, vmem],
        scratch_shapes=[
            pltpu.SMEM(pattern_one.shape[::-1], jnp.int32),
            pltpu.SMEM(parents.shape, jnp.int32),
            buffer(rows, CORES, owned, *block),
            buffer(rows, KINDS, *block),
            buffer(*block),
            buffer(CORES, chips, piece, width),
            buffer(CORES, chips, piece, width),
            buffer(chips, piece, width),
            buffer(rows, piece, width),
            buffer(KINDS, CORES * width, width),
            buffer(CORES, *block),
            buffer(CORES, *block),
            buffer(CORES, *block),
            buffer(CORES, *block),
            buffer(KINDS, *block),
            buffer(KINDS, chips, piece, width),
            buffer(rows, KINDS, piece, width),
            dma((owned + 6,)),
            dma((3, chips)),
            dma((3, chips)),
            dma((2, chips)),
            dma((2, chips)),
            dma((2,)),
            dma((2,)),
            dma((KINDS, rows)),
            dma((KINDS, rows)),
            dma((rows + KINDS, chips, 2 * chips)),
            dma((rows, chips, 2)),
            dma((2, rows, owned)),
            dma((rows, owned)),
            dma((rows, owned)),
            dma((rows, owned)),
            dma((2,)),
            dma((2,)),
            dma((2,)),
            dma((len(STRIPS), chips)),
            dma((len(STRIPS), chips)),
            dma((2, len(STRIPS), rows, rows)),
            dma((len(STRIPS), rows)),
            dma((len(STRIPS), rows)),
            dma((len(STRIPS), chips)),
        ],
        compiler_params=pltpu.CompilerParams(collective_id=0, has_side_effects=True),
    )(pattern_one.T, parents, anc_inverse, low_one, pivot_one, low_two, second_scaled_factor)
    return tuple(
        pl.pallas_call(
            finish_kernel,
            out_shape=[
                f32(CORES, *block),
                f32(1, *block),
                f32(CORES, *block),
                f32(1, *block),
                f32(1, *block),
            ],
            in_specs=[anywhere] * 5,
            out_specs=[anywhere] * 5,
            scratch_shapes=[
                buffer(CORES, *block),
                buffer(CORES, *block),
                buffer(KINDS, *block),
                buffer(*block),
                buffer(*block),
                dma((7,)),
                dma((5,)),
            ],
        )(column_one, column_two, final, pivot_one, second_pivot_inverse)
    )


def solution(mesh):
    placed = (
        P("pcol", "prow"),
        P(),
        P(),
        P("pcol", "prow", None),
        P("pcol", None, None),
        P("pcol", "prow", None),
        P("pcol", None, None),
        P("pcol", None, None),
    )
    return jax.shard_map(
        body,
        mesh=mesh,
        in_specs=placed,
        out_specs=(
            P("prow", "pcol", None),
            P("pcol", None, None),
            P("prow", "pcol", None),
            P("pcol", None, None),
            P("pcol", None, None),
        ),
        check_vma=False,
    )
```

```python
import functools

import jax
import jax.numpy as jnp
from jax import lax
from jax.experimental import pallas as pl
from jax.experimental.pallas import tpu as pltpu
from jax.sharding import PartitionSpec as P

MESH = pl.DeviceIdType.MESH
CORES = 2
UP, DOWN = 0, 1
LOW_ONE, LOW_TWO, LOW_PARENT = 0, 1, 2
DIAG, CROSS, SECOND = 0, 1, 2
KINDS = 3
PARTS = 1
STRIPS = [(kind, part) for kind in range(KINDS) for part in range(PARTS)]


def split(x):
    hi = x.astype(jnp.bfloat16)
    return hi, (x - hi.astype(jnp.float32)).astype(jnp.bfloat16)


def dot3(left, right, transposed=False):
    contract = (((0,), (0,)), ((), ())) if transposed else (((1,), (0,)), ((), ()))
    dot = functools.partial(
        lax.dot_general, dimension_numbers=contract, preferred_element_type=jnp.float32
    )
    return dot(left[0], right[1]) + dot(left[1], right[0]) + dot(left[0], right[0])


def fused_kernel(
    rows,
    cols,
    pattern_table,
    parents_table,
    anc,
    low_one,
    pivot_one,
    low_two,
    factor,
    out_one,
    out_two,
    final,
    pattern,
    parents,
    z,
    low,
    whole_factor,
    scattered,
    scattered_pivot,
    scattered_two,
    staged,
    sums,
    column,
    parent_column,
    product,
    column_two,
    partial,
    partials,
    reduced,
    load_sem,
    scatter_send,
    scatter_recv,
    factor_send,
    factor_recv,
    swap_send,
    swap_recv,
    low_send,
    low_recv,
    share_send,
    share_recv,
    z_send,
    z_recv,
    near_send,
    near_recv,
    column_send,
    column_recv,
    column_store,
    part_send,
    part_recv,
    line_send,
    line_recv,
    last_send,
    last_recv,
    keep_sem,
):
    row, col = lax.axis_index("prow"), lax.axis_index("pcol")
    chips = cols // CORES
    width = factor.shape[1]
    piece = width // chips
    owned = anc.shape[1] // width
    chip, core = col // CORES, lax.rem(col, CORES)
    other = 1 - core
    mine = row * CORES + core
    partner = (row, chip * CORES + other)

    def beside(p):
        return (row, p * CORES + core)

    def turn(start, d, size):
        return lax.rem(start + d + size, size)

    def rows_of(p):
        return pl.ds(pl.multiple_of(p * piece, piece), piece)

    strip = piece // PARTS

    def strip_of(p, part):
        return pl.ds(pl.multiple_of(p * piece + part * strip, strip), strip)

    def remote(source, target, send, recv, device):
        return pltpu.make_async_remote_copy(
            src_ref=source,
            dst_ref=target,
            send_sem=send,
            recv_sem=recv,
            device_id=device,
            device_id_type=MESH,
        )

    def order(t):
        below, above = row, rows - 1 - row
        both = 2 * jnp.minimum(below, above)
        paired = t <= both
        distance = jnp.where(paired, (t + 1) // 2, t - both // 2)
        up = jnp.where(paired, lax.rem(t, 2) == 1, above > below)
        return jnp.where(up, row + distance, row - distance)

    sent = []

    loads = [
        pltpu.make_async_copy(
            anc.at[:, pl.ds(b * width, width)], z.at[row, core, b], load_sem.at[b]
        )
        for b in range(owned)
    ]
    loads_low = [
        pltpu.make_async_copy(
            low_one.at[0, rows_of(chip)], scattered.at[core, chip], load_sem.at[owned]
        ),
        pltpu.make_async_copy(
            low_two.at[0, rows_of(chip)], scattered_two.at[chip], load_sem.at[owned + 1]
        ),
        pltpu.make_async_copy(
            pivot_one.at[0, rows_of(chip)], scattered_pivot.at[core, chip], load_sem.at[owned + 2]
        ),
    ]
    load_factor = pltpu.make_async_copy(factor.at[0], whole_factor, load_sem.at[owned + 3])
    loads_index = [
        pltpu.make_async_copy(pattern_table, pattern, load_sem.at[owned + 4]),
        pltpu.make_async_copy(parents_table, parents, load_sem.at[owned + 5]),
    ]
    for copy in loads_index + loads + loads_low:
        copy.start()

    @pl.when(chip == row)
    def _():
        load_factor.start()

    barrier = pltpu.get_barrier_semaphore()
    peers = [(turn(row, d, rows), col) for d in range(1, rows)]
    peers += [beside(turn(chip, d, chips)) for d in range(1, chips)] + [partner]
    for device in peers:
        pl.semaphore_signal(barrier, inc=1, device_id=device, device_id_type=MESH)
    pl.semaphore_wait(barrier, len(peers))

    def scatter(op, d, source, target, device):
        return remote(source, target, scatter_send.at[op, d], scatter_recv.at[op, d], device)

    scatters = [
        (low_one, scattered.at[core]),
        (low_two, scattered_two),
        (pivot_one, scattered_pivot.at[core]),
    ]
    swapped = [scattered, scattered_pivot]

    def scatter_all(op):
        source, target = scatters[op]
        for d in range(1, chips):
            p = turn(chip, d, chips)
            copy = scatter(op, d, source.at[0, rows_of(p)], target.at[chip], beside(p))
            copy.start()
            sent.append(copy)


    def z_line(source, b, direction):
        there = row + 1 if direction == UP else row - 1
        return remote(
            z.at[source, core, b],
            z.at[source, core, b],
            z_send.at[direction, source, b],
            z_recv.at[source, b],
            (there, col),
        )

    def z_near(source, b):
        return remote(
            z.at[source, core, b],
            z.at[source, core, b],
            near_send.at[source, b],
            near_recv.at[source, b],
            partner,
        )

    def z_near_arrival(source, b):
        target = z.at[source, other, b]
        return remote(target, target, near_send.at[source, b], near_recv.at[source, b], partner)

    def z_pass_on(source, b):
        @pl.when(jnp.logical_and(source <= row, row + 1 < rows))
        def _():
            z_line(source, b, UP).start()

        @pl.when(jnp.logical_and(source >= row, row > 0))
        def _():
            z_line(source, b, DOWN).start()

    def z_arrive(source, b):
        z_line(source, b, UP).wait_recv()
        z_pass_on(source, b)
        z_near(source, b).start()

    for b, copy in enumerate(loads):
        copy.wait()
        z_pass_on(row, b)

    scatter_all(0)
    scatter_all(1)
    for b in range(owned):
        z_near(row, b).start()

    def factor_piece(d, part, p):
        return remote(
            whole_factor.at[rows_of(part)],
            whole_factor.at[rows_of(part)],
            factor_send.at[0, d],
            factor_recv.at[0, d],
            beside(p),
        )

    def factor_first(d, p):
        return remote(
            factor.at[0, rows_of(p)],
            whole_factor.at[rows_of(p)],
            factor_send.at[1, d],
            factor_recv.at[1, 0],
            beside(p),
        )

    def arrivals(op, target):
        for d in range(1, chips):
            p = turn(chip, -d, chips)
            scatter(op, d, target.at[p], target.at[p], beside(p)).wait_recv()

    def swap(op):
        return remote(
            swapped[op].at[core],
            swapped[op].at[core],
            swap_send.at[op],
            swap_recv.at[op],
            partner,
        )

    def swap_arrival(op):
        return remote(
            swapped[op].at[other],
            swapped[op].at[other],
            swap_send.at[op],
            swap_recv.at[op],
            partner,
        )

    for copy in loads_low + loads_index:
        copy.wait()
    arrivals(0, scatters[0][1])
    swap(0).start()
    sent.append(swap(0))
    arrivals(1, scattered_two)
    swap_arrival(0).wait_recv()
    for plane in range(rows):
        parent = parents[plane * CORES + core]
        staged[plane] = scattered[lax.rem(parent, CORES), parent // CORES]

    def pieces_for(plane):
        return [scattered.at[core, plane], scattered_two.at[plane], staged.at[plane]]

    sources = [order(t) for t in range(rows)]
    for plane in sources[1:]:
        e = lax.rem(plane - row + rows, rows)
        for kind, source in enumerate(pieces_for(plane)):
            copy = remote(
                source,
                low.at[row, kind, rows_of(chip)],
                low_send.at[kind, e],
                low_recv.at[kind, e],
                (plane, col),
            )
            copy.start()
            sent.append(copy)

    masks = [1 << n for n in range((chips - 1).bit_length())]
    trees = [masks, masks[::-1]]
    offsets = sorted(range(1, chips), key=lambda o: o.bit_count())

    def flip(p, offset):
        for mask in masks:
            if offset & mask:
                p = p + mask - 2 * mask * lax.rem(p // mask, 2)
        return p

    def half_of(p, half):
        size = piece // 2
        return pl.ds(pl.multiple_of(p * piece + half * size, size), size)

    def share(source, offset, at, part, to, half):
        e = lax.rem(row - source + rows, rows)
        target = low.at[source, :, part]
        return remote(
            target, target, share_send.at[e, offset, at], share_recv.at[e, to, half], beside(flip(chip, offset))
        )

    def own_share(kind, source, mask):
        return remote(
            source,
            low.at[row, kind, rows_of(chip)],
            share_send.at[rows + kind, mask, 0],
            share_recv.at[0, mask, 0],
            beside(flip(chip, mask)),
        )

    def share_wait(source, offset, half):
        origin = flip(chip, offset)
        if offset not in masks:
            share(source, offset, 0, half_of(origin, half), offset, half).wait_recv()
        elif half == 0:
            share(source, offset, 0, rows_of(origin), offset, 0).wait_recv()

    def share_relay(source, last_hop):
        for offset in offsets:
            ways = [
                (half, tree[max(n for n, mask in enumerate(tree) if offset & mask) + 1 :])
                for half, tree in enumerate(trees)
            ]
            if last_hop != (not any(onward for _, onward in ways)):
                continue
            for half, onward in ways:
                share_wait(source, offset, half)
                for mask in onward:
                    copy = share(
                        source,
                        mask,
                        2 * offset + half,
                        half_of(flip(chip, offset), half),
                        offset ^ mask,
                        half,
                    )
                    copy.start()
                    sent.append(copy)

    def low_arrive(source):
        e = lax.rem(row - source + rows, rows)
        for kind in range(KINDS):
            target = low.at[source, kind, rows_of(chip)]
            remote(
                target, target, low_send.at[kind, e], low_recv.at[kind, e], (source, col)
            ).wait_recv()
        for mask in masks:
            copy = share(source, mask, 0, rows_of(chip), mask, 0)
            copy.start()
            sent.append(copy)

    for kind, source in enumerate(pieces_for(row)):
        for mask in masks:
            copy = own_share(kind, source, mask)
            copy.start()
            sent.append(copy)
    low[row, LOW_ONE, rows_of(chip)] = scattered[core, row]
    low[row, LOW_TWO, rows_of(chip)] = scattered_two[row]
    low[row, LOW_PARENT, rows_of(chip)] = staged[row]

    parent = parents[mine]

    def chosen(source, at):
        value = z[source, :, 0]
        for b in range(1, owned):
            value = jnp.where(at == b, z[source, :, b], value)
        return value.reshape(CORES * width, width)

    def store_column(at, buffer, out):
        keep = pltpu.make_async_copy(buffer.at[core], out.at[core], column_store.at[at])
        away = remote(
            buffer.at[other], out.at[core], column_send.at[at], column_recv.at[at], partner
        )
        keep.start()
        away.start()
        return keep, away

    def part_copy(kind, part, d, p, source, target):
        n = kind * PARTS + part
        return remote(source, target, part_send.at[n, d], part_recv.at[n, d], beside(p))

    def reduce_scatter(kind):
        for part in range(PARTS):
            for d in range(1, chips):
                p = turn(chip, d, chips)
                target = partials.at[kind, chip, strip_of(0, part)]
                copy = part_copy(kind, part, d, p, partial.at[kind, strip_of(p, part)], target)
                copy.start()
                sent.append(copy)

    slot_one = lax.rem(pattern[chip, mine], owned)
    slot_two = lax.rem(pattern[chip, parent], owned)
    stores = []

    def add_products(source, first_time=False, last_time=False):
        for b in range(owned):
            z_near_arrival(source, b).wait_recv()
        lhs = split(chosen(source, lax.rem(pattern[source, mine], owned)))
        first = dot3(lhs, split(low[source, LOW_ONE]))
        sums[0] = first if first_time else sums[0] + first
        if last_time:
            column[...] = -sums[0].reshape(CORES, width, width)
            partial[DIAG] = dot3(
                split(low[chip, LOW_ONE]), split(column[slot_one]), transposed=True
            )
            reduce_scatter(DIAG)
            stores.append(store_column(0, column, out_one))
        lhs = split(chosen(source, lax.rem(pattern[source, parent], owned)))
        second = dot3(lhs, split(low[source, LOW_PARENT]))
        third = dot3(lhs, split(low[source, LOW_TWO]))
        for n, value in enumerate([second, third], 1):
            sums[n] = value if first_time else sums[n] + value

    @pl.when(chip == row)
    def _():
        load_factor.wait()
        for d in range(1, chips):
            p = turn(chip, d, chips)
            factor_first(d, p).start()
            factor_piece(d, chip, p).start()

    scatter_all(2)
    inner = jnp.logical_and(row > 0, row + 1 < rows)

    @pl.when(inner)
    def _():
        for b in range(owned):
            for source in sources[1:3]:
                z_arrive(source, b)

    @pl.when(jnp.logical_not(inner))
    def _():
        for b in range(owned):
            z_arrive(sources[1], b)

    share_relay(row, False)
    low_arrive(sources[1])
    low_arrive(sources[2])
    share_relay(sources[1], False)
    for source in sources[3:]:
        low_arrive(source)
    @pl.when(inner)
    def _():
        for source in sources[3:]:
            z_arrive(source, 0)

    for source in sources[2:]:
        share_relay(source, False)

    @pl.when(inner)
    def _():
        for source in sources[3:]:
            for b in range(1, owned):
                z_arrive(source, b)

    @pl.when(chip != row)
    def _():
        factor_first(0, chip).wait_recv()
        for d in range(1, chips):
            p = turn(chip, d, chips)

            @pl.when(p != row)
            def _():
                factor_piece(d, chip, p).start()

    share_relay(row, True)
    add_products(row, True)
    share_relay(sources[1], True)
    add_products(sources[1])
    arrivals(2, scatters[2][1])
    swap(1).start()
    sent.append(swap(1))
    for source in sources[2:]:
        share_relay(source, True)

        @pl.when(jnp.logical_not(inner))
        def _():
            for b in range(owned):
                z_arrive(source, b)

        add_products(source, last_time=source is sources[-1])

    @pl.when(chip != row)
    def _():
        for d in range(1, chips):
            factor_piece(d, turn(chip, -d, chips), partner[1]).wait_recv()


    swap_arrival(1).wait_recv()
    whole = split(whole_factor[...])
    parent_column[...] = -sums[1].reshape(CORES, width, width)
    scaled = dot3(split(-sums[1]), whole)
    product[...] = scaled.reshape(CORES, width, width)
    column_two[...] = -(scaled + sums[2]).reshape(CORES, width, width)
    two_split = split(low[chip, LOW_TWO])
    cross = dot3(split(low[chip, LOW_PARENT]), split(product[slot_two]), transposed=True)
    cross = cross - dot3(split(parent_column[slot_two]), two_split, transposed=True)
    partial[CROSS] = cross
    pivot_rows = scattered_pivot[lax.rem(parent, CORES), parent // CORES]
    partial[CROSS, rows_of(chip)] -= dot3(split(pivot_rows), whole)
    stores.append(store_column(1, column_two, out_two))
    reduce_scatter(CROSS)
    partial[SECOND] = dot3(two_split, split(column_two[slot_two]), transposed=True) + dot3(
        whole, split(partial[CROSS]), transposed=True
    )
    reduce_scatter(SECOND)

    def line(kind, part, source, distance):
        way = UP if distance > 0 else DOWN
        n = kind * PARTS + part
        block = reduced.at[source, kind, strip_of(0, part)]
        return remote(
            block,
            block,
            line_send.at[way, n, source, abs(distance) - 1],
            line_recv.at[n, source],
            (row + distance, col),
        )

    def own_onward(kind, act):
        for distance in range(1, rows, 2):

            @pl.when(row + distance < rows)
            def _():
                act(distance)

            @pl.when(row >= distance)
            def _():
                act(-distance)

    def relay_onward(kind, source, act):
        odd = lax.rem(row + source, 2) == 1

        @pl.when(jnp.logical_and(odd, jnp.logical_and(source < row, row + 1 < rows)))
        def _():
            act(1)

        @pl.when(jnp.logical_and(odd, jnp.logical_and(source > row, row > 0)))
        def _():
            act(-1)

    def last(kind, part, source):
        n = kind * PARTS + part
        d = lax.rem(source - chip + chips, chips)
        return remote(
            reduced.at[source, kind, strip_of(0, part)],
            final.at[kind, strip_of(chip, part)],
            last_send.at[n, source],
            last_recv.at[n, d],
            beside(source),
        )

    def keep_sum(kind, part):
        return pltpu.make_async_copy(
            reduced.at[chip, kind, strip_of(0, part)],
            final.at[kind, strip_of(chip, part)],
            keep_sem.at[kind * PARTS + part],
        )

    def hand_on(kind, part, source):
        @pl.when(source != chip)
        def _():
            last(kind, part, source).start()

        @pl.when(source == chip)
        def _():
            keep_sum(kind, part).start()

    for kind, part in STRIPS:
        total = partial[kind, strip_of(chip, part)]
        for d in range(1, chips):
            p = turn(chip, -d, chips)
            target = partials.at[kind, p, strip_of(0, part)]
            part_copy(kind, part, d, p, target, target).wait_recv()
            total += partials[kind, p, strip_of(0, part)]
        reduced[row, kind, strip_of(0, part)] = total
        own_onward(kind, lambda distance: line(kind, part, row, distance).start())
        hand_on(kind, part, row)

    def spread(kind, part, source):
        @pl.when(source != row)
        def _():
            line(kind, part, source, 1).wait_recv()
            relay_onward(
                kind, source, lambda distance: line(kind, part, source, distance).start()
            )
            hand_on(kind, part, source)

    for source in range(1, rows - 1):
        for kind, part in STRIPS:
            spread(kind, part, source)
    near_end = jnp.where(2 * row < rows, 0, rows - 1)
    lag = PARTS
    for n in range(len(STRIPS) + lag):
        if n < len(STRIPS):
            spread(*STRIPS[n], near_end)
        if n >= lag:
            spread(*STRIPS[n - lag], rows - 1 - near_end)

    for keep, away in stores:
        keep.wait()
        away.wait_send()
        away.wait_recv()
    for copy in sent:
        copy.wait_send()

    @pl.when(chip == row)
    def _():
        for d in range(1, chips):
            p = turn(chip, d, chips)
            factor_first(d, p).wait_send()
            factor_piece(d, chip, p).wait_send()

    @pl.when(chip != row)
    def _():
        for d in range(1, chips):
            p = turn(chip, d, chips)

            @pl.when(p != row)
            def _():
                factor_piece(d, chip, p).wait_send()

    def drain(source, carry):
        for b in range(owned):
            z_near(source, b).wait_send()
        @pl.when(jnp.logical_and(source <= row, row + 1 < rows))
        def _():
            for b in range(owned):
                z_line(source, b, UP).wait_send()

        @pl.when(jnp.logical_and(source >= row, row > 0))
        def _():
            for b in range(owned):
                z_line(source, b, DOWN).wait_send()

        for kind, part in STRIPS:
            relay_onward(
                kind, source, lambda distance: line(kind, part, source, distance).wait_send()
            )

        @pl.when(source != chip)
        def _():
            for kind, part in STRIPS:
                last(kind, part, source).wait_send()

        return carry

    lax.fori_loop(0, rows, drain, 0)
    for kind, part in STRIPS:
        own_onward(kind, lambda distance: line(kind, part, row, distance).wait_send())

    for kind, part in STRIPS:
        keep_sum(kind, part).wait()
    for kind, part in STRIPS:
        for d in range(1, chips):
            p = turn(chip, -d, chips)
            target = final.at[kind, strip_of(p, part)]
            n = kind * PARTS + part
            remote(
                target, target, last_send.at[n, 0], last_recv.at[n, d], beside(p)
            ).wait_recv()


def finish_kernel(
    column_one,
    column_two,
    final,
    pivot_one,
    pivot_two,
    out_one,
    out_diag,
    out_two,
    out_cross,
    out_second,
    one,
    two,
    sums,
    diag,
    second,
    load_sem,
    store_sem,
):
    sources = [column_one, column_two, final.at[CROSS], pivot_one.at[0], final.at[DIAG]]
    sources += [pivot_two.at[0], final.at[SECOND]]
    places = [one, two, sums.at[CROSS], diag, sums.at[DIAG], second, sums.at[SECOND]]
    loads = [
        pltpu.make_async_copy(source, place, load_sem.at[n])
        for n, (source, place) in enumerate(zip(sources, places))
    ]
    kept = [(one, out_one), (two, out_two), (sums.at[CROSS], out_cross.at[0])]
    kept += [(diag, out_diag.at[0]), (second, out_second.at[0])]
    stores = [
        pltpu.make_async_copy(place, out, store_sem.at[n]) for n, (place, out) in enumerate(kept)
    ]
    for copy in loads:
        copy.start()
    for n in range(3):
        loads[n].wait()
        stores[n].start()
    loads[3].wait()
    loads[4].wait()
    diag[...] = diag[...] - sums[DIAG]
    stores[3].start()
    loads[5].wait()
    loads[6].wait()
    second[...] = second[...] - sums[SECOND]
    stores[4].start()
    for copy in stores:
        copy.wait()


def body(
    anc_inverse,
    pattern_one,
    parents,
    low_one,
    pivot_one,
    low_two,
    second_scaled_factor,
    second_pivot_inverse,
):
    rows, cols = lax.axis_size("prow"), lax.axis_size("pcol")
    width = pivot_one.shape[1]
    chips = cols // CORES
    owned = anc_inverse.shape[1] // width
    piece = width // chips
    if rows != chips:
        raise ValueError("mesh shape")
    anywhere = pl.BlockSpec(memory_space=pl.ANY)

    def f32(*shape):
        return jax.ShapeDtypeStruct(shape, jnp.float32)

    def buffer(*shape):
        return pltpu.VMEM(shape, jnp.float32)

    dma = pltpu.SemaphoreType.DMA
    block = (width, width)
    column_one, column_two, final = pl.pallas_call(
        functools.partial(fused_kernel, rows, cols),
        out_shape=[f32(CORES, *block), f32(CORES, *block), f32(KINDS, *block)],
        in_specs=[anywhere] * 7,
        out_specs=[anywhere, anywhere, anywhere],
        scratch_shapes=[
            pltpu.SMEM(pattern_one.shape[::-1], jnp.int32),
            pltpu.SMEM(parents.shape, jnp.int32),
            buffer(rows, CORES, owned, *block),
            buffer(rows, KINDS, *block),
            buffer(*block),
            buffer(CORES, chips, piece, width),
            buffer(CORES, chips, piece, width),
            buffer(chips, piece, width),
            buffer(rows, piece, width),
            buffer(KINDS, CORES * width, width),
            buffer(CORES, *block),
            buffer(CORES, *block),
            buffer(CORES, *block),
            buffer(CORES, *block),
            buffer(KINDS, *block),
            buffer(KINDS, chips, piece, width),
            buffer(rows, KINDS, piece, width),
            dma((owned + 6,)),
            dma((3, chips)),
            dma((3, chips)),
            dma((2, chips)),
            dma((2, chips)),
            dma((2,)),
            dma((2,)),
            dma((KINDS, rows)),
            dma((KINDS, rows)),
            dma((rows + KINDS, chips, 2 * chips)),
            dma((rows, chips, 2)),
            dma((2, rows, owned)),
            dma((rows, owned)),
            dma((rows, owned)),
            dma((rows, owned)),
            dma((2,)),
            dma((2,)),
            dma((2,)),
            dma((len(STRIPS), chips)),
            dma((len(STRIPS), chips)),
            dma((2, len(STRIPS), rows, rows)),
            dma((len(STRIPS), rows)),
            dma((len(STRIPS), rows)),
            dma((len(STRIPS), chips)),
            dma((len(STRIPS),)),
        ],
        compiler_params=pltpu.CompilerParams(collective_id=0, has_side_effects=True),
    )(pattern_one.T, parents, anc_inverse, low_one, pivot_one, low_two, second_scaled_factor)
    return tuple(
        pl.pallas_call(
            finish_kernel,
            out_shape=[
                f32(CORES, *block),
                f32(1, *block),
                f32(CORES, *block),
                f32(1, *block),
                f32(1, *block),
            ],
            in_specs=[anywhere] * 5,
            out_specs=[anywhere] * 5,
            scratch_shapes=[
                buffer(CORES, *block),
                buffer(CORES, *block),
                buffer(KINDS, *block),
                buffer(*block),
                buffer(*block),
                dma((7,)),
                dma((5,)),
            ],
        )(column_one, column_two, final, pivot_one, second_pivot_inverse)
    )


def solution(mesh):
    placed = (
        P("pcol", "prow"),
        P(),
        P(),
        P("pcol", "prow", None),
        P("pcol", None, None),
        P("pcol", "prow", None),
        P("pcol", None, None),
        P("pcol", None, None),
    )
    return jax.shard_map(
        body,
        mesh=mesh,
        in_specs=placed,
        out_specs=(
            P("prow", "pcol", None),
            P("pcol", None, None),
            P("prow", "pcol", None),
            P("pcol", None, None),
            P("pcol", None, None),
        ),
        check_vma=False,
    )
```

```python
import functools

import jax
import jax.numpy as jnp
from jax import lax
from jax.experimental import pallas as pl
from jax.experimental.pallas import tpu as pltpu
from jax.sharding import PartitionSpec as P

MESH = pl.DeviceIdType.MESH
CORES = 2
UP, DOWN = 0, 1
LOW_ONE, LOW_TWO, LOW_PARENT = 0, 1, 2
DIAG, CROSS, SECOND = 0, 1, 2
KINDS = 3
PARTS = 1
STRIPS = [(kind, part) for kind in range(KINDS) for part in range(PARTS)]


def split(x):
    hi = x.astype(jnp.bfloat16)
    return hi, (x - hi.astype(jnp.float32)).astype(jnp.bfloat16)


def dot3(left, right, transposed=False):
    contract = (((0,), (0,)), ((), ())) if transposed else (((1,), (0,)), ((), ()))
    dot = functools.partial(
        lax.dot_general, dimension_numbers=contract, preferred_element_type=jnp.float32
    )
    return dot(left[0], right[1]) + dot(left[1], right[0]) + dot(left[0], right[0])


def fused_kernel(
    rows,
    cols,
    pattern_table,
    parents_table,
    anc,
    low_one,
    pivot_one,
    low_two,
    factor,
    pivot_two,
    out_one,
    out_two,
    final,
    pattern,
    parents,
    z,
    low,
    whole_factor,
    pivot_own,
    pivot_second,
    scattered,
    scattered_pivot,
    scattered_two,
    staged,
    sums,
    column,
    parent_column,
    product,
    column_two,
    partial,
    partials,
    reduced,
    load_sem,
    scatter_send,
    scatter_recv,
    factor_send,
    factor_recv,
    swap_send,
    swap_recv,
    low_send,
    low_recv,
    share_send,
    share_recv,
    z_send,
    z_recv,
    near_send,
    near_recv,
    column_send,
    column_recv,
    column_store,
    part_send,
    part_recv,
    line_send,
    line_recv,
    last_send,
    last_recv,
    keep_sem,
):
    row, col = lax.axis_index("prow"), lax.axis_index("pcol")
    chips = cols // CORES
    width = factor.shape[1]
    piece = width // chips
    owned = anc.shape[1] // width
    chip, core = col // CORES, lax.rem(col, CORES)
    other = 1 - core
    mine = row * CORES + core
    partner = (row, chip * CORES + other)

    def beside(p):
        return (row, p * CORES + core)

    def turn(start, d, size):
        return lax.rem(start + d + size, size)

    def rows_of(p):
        return pl.ds(pl.multiple_of(p * piece, piece), piece)

    strip = piece // PARTS

    def strip_of(p, part):
        return pl.ds(pl.multiple_of(p * piece + part * strip, strip), strip)

    def remote(source, target, send, recv, device):
        return pltpu.make_async_remote_copy(
            src_ref=source,
            dst_ref=target,
            send_sem=send,
            recv_sem=recv,
            device_id=device,
            device_id_type=MESH,
        )

    def order(t):
        below, above = row, rows - 1 - row
        both = 2 * jnp.minimum(below, above)
        paired = t <= both
        distance = jnp.where(paired, (t + 1) // 2, t - both // 2)
        up = jnp.where(paired, lax.rem(t, 2) == 1, above > below)
        return jnp.where(up, row + distance, row - distance)

    sent = []

    loads = [
        pltpu.make_async_copy(
            anc.at[:, pl.ds(b * width, width)], z.at[row, core, b], load_sem.at[b]
        )
        for b in range(owned)
    ]
    loads_low = [
        pltpu.make_async_copy(
            low_one.at[0, rows_of(chip)], scattered.at[core, chip], load_sem.at[owned]
        ),
        pltpu.make_async_copy(
            low_two.at[0, rows_of(chip)], scattered_two.at[chip], load_sem.at[owned + 1]
        ),
        pltpu.make_async_copy(
            pivot_one.at[0, rows_of(chip)], scattered_pivot.at[core, chip], load_sem.at[owned + 2]
        ),
    ]
    loads_pivot = [
        pltpu.make_async_copy(pivot_one.at[0], pivot_own, load_sem.at[owned + 6]),
        pltpu.make_async_copy(pivot_two.at[0], pivot_second, load_sem.at[owned + 7]),
    ]
    load_factor = pltpu.make_async_copy(factor.at[0], whole_factor, load_sem.at[owned + 3])
    loads_index = [
        pltpu.make_async_copy(pattern_table, pattern, load_sem.at[owned + 4]),
        pltpu.make_async_copy(parents_table, parents, load_sem.at[owned + 5]),
    ]
    for copy in loads_index + loads + loads_low + loads_pivot:
        copy.start()

    @pl.when(chip == row)
    def _():
        load_factor.start()

    barrier = pltpu.get_barrier_semaphore()
    peers = [(turn(row, d, rows), col) for d in range(1, rows)]
    peers += [beside(turn(chip, d, chips)) for d in range(1, chips)] + [partner]
    for device in peers:
        pl.semaphore_signal(barrier, inc=1, device_id=device, device_id_type=MESH)
    pl.semaphore_wait(barrier, len(peers))

    def scatter(op, d, source, target, device):
        return remote(source, target, scatter_send.at[op, d], scatter_recv.at[op, d], device)

    scatters = [
        (low_one, scattered.at[core]),
        (low_two, scattered_two),
        (pivot_one, scattered_pivot.at[core]),
    ]
    swapped = [scattered, scattered_pivot]

    def scatter_all(op):
        source, target = scatters[op]
        for d in range(1, chips):
            p = turn(chip, d, chips)
            copy = scatter(op, d, source.at[0, rows_of(p)], target.at[chip], beside(p))
            copy.start()
            sent.append(copy)


    def z_line(source, b, direction):
        there = row + 1 if direction == UP else row - 1
        return remote(
            z.at[source, core, b],
            z.at[source, core, b],
            z_send.at[direction, source, b],
            z_recv.at[source, b],
            (there, col),
        )

    def z_near(source, b):
        return remote(
            z.at[source, core, b],
            z.at[source, core, b],
            near_send.at[source, b],
            near_recv.at[source, b],
            partner,
        )

    def z_near_arrival(source, b):
        target = z.at[source, other, b]
        return remote(target, target, near_send.at[source, b], near_recv.at[source, b], partner)

    def z_pass_on(source, b):
        @pl.when(jnp.logical_and(source <= row, row + 1 < rows))
        def _():
            z_line(source, b, UP).start()

        @pl.when(jnp.logical_and(source >= row, row > 0))
        def _():
            z_line(source, b, DOWN).start()

    def z_arrive(source, b):
        z_line(source, b, UP).wait_recv()
        z_pass_on(source, b)
        z_near(source, b).start()

    for b, copy in enumerate(loads):
        copy.wait()
        z_pass_on(row, b)

    scatter_all(0)
    scatter_all(1)
    for b in range(owned):
        z_near(row, b).start()

    def factor_piece(d, part, p):
        return remote(
            whole_factor.at[rows_of(part)],
            whole_factor.at[rows_of(part)],
            factor_send.at[0, d],
            factor_recv.at[0, d],
            beside(p),
        )

    def factor_first(d, p):
        return remote(
            factor.at[0, rows_of(p)],
            whole_factor.at[rows_of(p)],
            factor_send.at[1, d],
            factor_recv.at[1, 0],
            beside(p),
        )

    def arrivals(op, target):
        for d in range(1, chips):
            p = turn(chip, -d, chips)
            scatter(op, d, target.at[p], target.at[p], beside(p)).wait_recv()

    def swap(op):
        return remote(
            swapped[op].at[core],
            swapped[op].at[core],
            swap_send.at[op],
            swap_recv.at[op],
            partner,
        )

    def swap_arrival(op):
        return remote(
            swapped[op].at[other],
            swapped[op].at[other],
            swap_send.at[op],
            swap_recv.at[op],
            partner,
        )

    for copy in loads_low + loads_index:
        copy.wait()
    arrivals(0, scatters[0][1])
    swap(0).start()
    sent.append(swap(0))
    arrivals(1, scattered_two)
    swap_arrival(0).wait_recv()
    for plane in range(rows):
        parent = parents[plane * CORES + core]
        staged[plane] = scattered[lax.rem(parent, CORES), parent // CORES]

    def pieces_for(plane):
        return [scattered.at[core, plane], scattered_two.at[plane], staged.at[plane]]

    sources = [order(t) for t in range(rows)]
    for plane in sources[1:]:
        e = lax.rem(plane - row + rows, rows)
        for kind, source in enumerate(pieces_for(plane)):
            copy = remote(
                source,
                low.at[row, kind, rows_of(chip)],
                low_send.at[kind, e],
                low_recv.at[kind, e],
                (plane, col),
            )
            copy.start()
            sent.append(copy)

    masks = [1 << n for n in range((chips - 1).bit_length())]
    trees = [masks, masks[::-1]]
    offsets = sorted(range(1, chips), key=lambda o: o.bit_count())

    def flip(p, offset):
        for mask in masks:
            if offset & mask:
                p = p + mask - 2 * mask * lax.rem(p // mask, 2)
        return p

    def half_of(p, half):
        size = piece // 2
        return pl.ds(pl.multiple_of(p * piece + half * size, size), size)

    def share(source, offset, at, part, to, half):
        e = lax.rem(row - source + rows, rows)
        target = low.at[source, :, part]
        return remote(
            target, target, share_send.at[e, offset, at], share_recv.at[e, to, half], beside(flip(chip, offset))
        )

    def own_share(kind, source, mask):
        return remote(
            source,
            low.at[row, kind, rows_of(chip)],
            share_send.at[rows + kind, mask, 0],
            share_recv.at[0, mask, 0],
            beside(flip(chip, mask)),
        )

    def share_wait(source, offset, half):
        origin = flip(chip, offset)
        if offset not in masks:
            share(source, offset, 0, half_of(origin, half), offset, half).wait_recv()
        elif half == 0:
            share(source, offset, 0, rows_of(origin), offset, 0).wait_recv()

    def share_relay(source, last_hop):
        for offset in offsets:
            ways = [
                (half, tree[max(n for n, mask in enumerate(tree) if offset & mask) + 1 :])
                for half, tree in enumerate(trees)
            ]
            if last_hop != (not any(onward for _, onward in ways)):
                continue
            for half, onward in ways:
                share_wait(source, offset, half)
                for mask in onward:
                    copy = share(
                        source,
                        mask,
                        2 * offset + half,
                        half_of(flip(chip, offset), half),
                        offset ^ mask,
                        half,
                    )
                    copy.start()
                    sent.append(copy)

    def low_arrive(source):
        e = lax.rem(row - source + rows, rows)
        for kind in range(KINDS):
            target = low.at[source, kind, rows_of(chip)]
            remote(
                target, target, low_send.at[kind, e], low_recv.at[kind, e], (source, col)
            ).wait_recv()
        for mask in masks:
            copy = share(source, mask, 0, rows_of(chip), mask, 0)
            copy.start()
            sent.append(copy)

    for kind, source in enumerate(pieces_for(row)):
        for mask in masks:
            copy = own_share(kind, source, mask)
            copy.start()
            sent.append(copy)
    low[row, LOW_ONE, rows_of(chip)] = scattered[core, row]
    low[row, LOW_TWO, rows_of(chip)] = scattered_two[row]
    low[row, LOW_PARENT, rows_of(chip)] = staged[row]

    parent = parents[mine]

    def chosen(source, at):
        value = z[source, :, 0]
        for b in range(1, owned):
            value = jnp.where(at == b, z[source, :, b], value)
        return value.reshape(CORES * width, width)

    def store_column(at, buffer, out):
        keep = pltpu.make_async_copy(buffer.at[core], out.at[core], column_store.at[at])
        away = remote(
            buffer.at[other], out.at[core], column_send.at[at], column_recv.at[at], partner
        )
        keep.start()
        away.start()
        return keep, away

    def part_copy(kind, part, d, p, source, target):
        n = kind * PARTS + part
        return remote(source, target, part_send.at[n, d], part_recv.at[n, d], beside(p))

    def reduce_scatter(kind):
        for part in range(PARTS):
            for d in range(1, chips):
                p = turn(chip, d, chips)
                target = partials.at[kind, chip, strip_of(0, part)]
                copy = part_copy(kind, part, d, p, partial.at[kind, strip_of(p, part)], target)
                copy.start()
                sent.append(copy)

    slot_one = lax.rem(pattern[chip, mine], owned)
    slot_two = lax.rem(pattern[chip, parent], owned)
    stores = []

    def add_products(source, first_time=False, last_time=False):
        for b in range(owned):
            z_near_arrival(source, b).wait_recv()
        lhs = split(chosen(source, lax.rem(pattern[source, mine], owned)))
        first = dot3(lhs, split(low[source, LOW_ONE]))
        sums[0] = first if first_time else sums[0] + first
        if last_time:
            column[...] = -sums[0].reshape(CORES, width, width)
            partial[DIAG] = dot3(
                split(low[chip, LOW_ONE]), split(column[slot_one]), transposed=True
            )
            reduce_scatter(DIAG)
            stores.append(store_column(0, column, out_one))
        lhs = split(chosen(source, lax.rem(pattern[source, parent], owned)))
        second = dot3(lhs, split(low[source, LOW_PARENT]))
        third = dot3(lhs, split(low[source, LOW_TWO]))
        for n, value in enumerate([second, third], 1):
            sums[n] = value if first_time else sums[n] + value

    @pl.when(chip == row)
    def _():
        load_factor.wait()
        for d in range(1, chips):
            p = turn(chip, d, chips)
            factor_first(d, p).start()
            factor_piece(d, chip, p).start()

    scatter_all(2)
    inner = jnp.logical_and(row > 0, row + 1 < rows)

    @pl.when(inner)
    def _():
        for b in range(owned):
            for source in sources[1:3]:
                z_arrive(source, b)

    @pl.when(jnp.logical_not(inner))
    def _():
        for b in range(owned):
            z_arrive(sources[1], b)

    share_relay(row, False)
    low_arrive(sources[1])
    low_arrive(sources[2])
    share_relay(sources[1], False)
    for source in sources[3:]:
        low_arrive(source)
    @pl.when(inner)
    def _():
        for source in sources[3:]:
            z_arrive(source, 0)

    for source in sources[2:]:
        share_relay(source, False)

    @pl.when(inner)
    def _():
        for source in sources[3:]:
            for b in range(1, owned):
                z_arrive(source, b)

    @pl.when(chip != row)
    def _():
        factor_first(0, chip).wait_recv()
        for d in range(1, chips):
            p = turn(chip, d, chips)

            @pl.when(p != row)
            def _():
                factor_piece(d, chip, p).start()

    share_relay(row, True)
    add_products(row, True)
    share_relay(sources[1], True)
    add_products(sources[1])
    arrivals(2, scatters[2][1])
    swap(1).start()
    sent.append(swap(1))
    for source in sources[2:]:
        share_relay(source, True)

        @pl.when(jnp.logical_not(inner))
        def _():
            for b in range(owned):
                z_arrive(source, b)

        add_products(source, last_time=source is sources[-1])

    @pl.when(chip != row)
    def _():
        for d in range(1, chips):
            factor_piece(d, turn(chip, -d, chips), partner[1]).wait_recv()


    swap_arrival(1).wait_recv()
    whole = split(whole_factor[...])
    parent_column[...] = -sums[1].reshape(CORES, width, width)
    scaled = dot3(split(-sums[1]), whole)
    product[...] = scaled.reshape(CORES, width, width)
    column_two[...] = -(scaled + sums[2]).reshape(CORES, width, width)
    two_split = split(low[chip, LOW_TWO])
    cross = dot3(split(low[chip, LOW_PARENT]), split(product[slot_two]), transposed=True)
    cross = cross - dot3(split(parent_column[slot_two]), two_split, transposed=True)
    partial[CROSS] = cross
    pivot_rows = scattered_pivot[lax.rem(parent, CORES), parent // CORES]
    partial[CROSS, rows_of(chip)] -= dot3(split(pivot_rows), whole)
    stores.append(store_column(1, column_two, out_two))
    reduce_scatter(CROSS)
    partial[SECOND] = dot3(two_split, split(column_two[slot_two]), transposed=True) + dot3(
        whole, split(partial[CROSS]), transposed=True
    )
    reduce_scatter(SECOND)

    def line(kind, part, source, distance):
        way = UP if distance > 0 else DOWN
        n = kind * PARTS + part
        block = reduced.at[source, kind, strip_of(0, part)]
        return remote(
            block,
            block,
            line_send.at[way, n, source, abs(distance) - 1],
            line_recv.at[n, source],
            (row + distance, col),
        )

    def own_onward(kind, act):
        for distance in range(1, rows, 2):

            @pl.when(row + distance < rows)
            def _():
                act(distance)

            @pl.when(row >= distance)
            def _():
                act(-distance)

    def relay_onward(kind, source, act):
        odd = lax.rem(row + source, 2) == 1

        @pl.when(jnp.logical_and(odd, jnp.logical_and(source < row, row + 1 < rows)))
        def _():
            act(1)

        @pl.when(jnp.logical_and(odd, jnp.logical_and(source > row, row > 0)))
        def _():
            act(-1)

    def last(kind, part, source):
        n = kind * PARTS + part
        d = lax.rem(source - chip + chips, chips)
        return remote(
            reduced.at[source, kind, strip_of(0, part)],
            final.at[kind, strip_of(chip, part)],
            last_send.at[n, source],
            last_recv.at[n, d],
            beside(source),
        )

    def keep_sum(kind, part):
        return pltpu.make_async_copy(
            reduced.at[chip, kind, strip_of(0, part)],
            final.at[kind, strip_of(chip, part)],
            keep_sem.at[kind * PARTS + part],
        )

    def hand_on(kind, part, source):
        @pl.when(source != chip)
        def _():
            last(kind, part, source).start()

        @pl.when(source == chip)
        def _():
            keep_sum(kind, part).start()

    for kind, part in STRIPS:
        total = partial[kind, strip_of(chip, part)]
        for d in range(1, chips):
            p = turn(chip, -d, chips)
            target = partials.at[kind, p, strip_of(0, part)]
            part_copy(kind, part, d, p, target, target).wait_recv()
            total += partials[kind, p, strip_of(0, part)]
        reduced[row, kind, strip_of(0, part)] = total
        own_onward(kind, lambda distance: line(kind, part, row, distance).start())
        hand_on(kind, part, row)

    def spread(kind, part, source):
        @pl.when(source != row)
        def _():
            line(kind, part, source, 1).wait_recv()
            relay_onward(
                kind, source, lambda distance: line(kind, part, source, distance).start()
            )
            hand_on(kind, part, source)

    for source in range(1, rows - 1):
        for kind, part in STRIPS:
            spread(kind, part, source)
    near_end = jnp.where(2 * row < rows, 0, rows - 1)
    lag = PARTS
    for n in range(len(STRIPS) + lag):
        if n < len(STRIPS):
            spread(*STRIPS[n], near_end)
        if n >= lag:
            spread(*STRIPS[n - lag], rows - 1 - near_end)

    for keep, away in stores:
        keep.wait()
        away.wait_send()
        away.wait_recv()
    for copy in sent:
        copy.wait_send()

    @pl.when(chip == row)
    def _():
        for d in range(1, chips):
            p = turn(chip, d, chips)
            factor_first(d, p).wait_send()
            factor_piece(d, chip, p).wait_send()

    @pl.when(chip != row)
    def _():
        for d in range(1, chips):
            p = turn(chip, d, chips)

            @pl.when(p != row)
            def _():
                factor_piece(d, chip, p).wait_send()

    def drain(source, carry):
        for b in range(owned):
            z_near(source, b).wait_send()
        @pl.when(jnp.logical_and(source <= row, row + 1 < rows))
        def _():
            for b in range(owned):
                z_line(source, b, UP).wait_send()

        @pl.when(jnp.logical_and(source >= row, row > 0))
        def _():
            for b in range(owned):
                z_line(source, b, DOWN).wait_send()

        for kind, part in STRIPS:
            relay_onward(
                kind, source, lambda distance: line(kind, part, source, distance).wait_send()
            )

        @pl.when(source != chip)
        def _():
            for kind, part in STRIPS:
                last(kind, part, source).wait_send()

        return carry

    lax.fori_loop(0, rows, drain, 0)
    for kind, part in STRIPS:
        own_onward(kind, lambda distance: line(kind, part, row, distance).wait_send())

    for copy in loads_pivot:
        copy.wait()
    for kind, part in STRIPS:
        keep_sum(kind, part).wait()
        for d in range(1, chips):
            p = turn(chip, -d, chips)
            target = final.at[kind, strip_of(p, part)]
            n = kind * PARTS + part
            remote(
                target, target, last_send.at[n, 0], last_recv.at[n, d], beside(p)
            ).wait_recv()
        if part == PARTS - 1 and kind in (DIAG, SECOND):
            pivot = pivot_own if kind == DIAG else pivot_second
            final[kind] = pivot[...] - final[kind]


def finish_kernel(
    column_one, column_two, final, out_one, out_diag, out_two, out_cross, out_second, store_sem
):
    kept = [(column_one, out_one), (column_two, out_two), (final.at[DIAG], out_diag.at[0])]
    kept += [(final.at[CROSS], out_cross.at[0]), (final.at[SECOND], out_second.at[0])]
    stores = [
        pltpu.make_async_copy(place, out, store_sem.at[n]) for n, (place, out) in enumerate(kept)
    ]
    for copy in stores:
        copy.start()
    for copy in stores:
        copy.wait()


def body(
    anc_inverse,
    pattern_one,
    parents,
    low_one,
    pivot_one,
    low_two,
    second_scaled_factor,
    second_pivot_inverse,
):
    rows, cols = lax.axis_size("prow"), lax.axis_size("pcol")
    width = pivot_one.shape[1]
    chips = cols // CORES
    owned = anc_inverse.shape[1] // width
    piece = width // chips
    if rows != chips:
        raise ValueError("mesh shape")
    anywhere = pl.BlockSpec(memory_space=pl.ANY)
    vmem = pl.BlockSpec(memory_space=pltpu.VMEM)

    def f32(*shape):
        return jax.ShapeDtypeStruct(shape, jnp.float32)

    def buffer(*shape):
        return pltpu.VMEM(shape, jnp.float32)

    dma = pltpu.SemaphoreType.DMA
    block = (width, width)
    column_one, column_two, final = pl.pallas_call(
        functools.partial(fused_kernel, rows, cols),
        out_shape=[buffer(CORES, *block), buffer(CORES, *block), buffer(KINDS, *block)],
        in_specs=[anywhere] * 8,
        out_specs=[vmem, vmem, vmem],
        scratch_shapes=[
            pltpu.SMEM(pattern_one.shape[::-1], jnp.int32),
            pltpu.SMEM(parents.shape, jnp.int32),
            buffer(rows, CORES, owned, *block),
            buffer(rows, KINDS, *block),
            buffer(*block),
            buffer(*block),
            buffer(*block),
            buffer(CORES, chips, piece, width),
            buffer(CORES, chips, piece, width),
            buffer(chips, piece, width),
            buffer(rows, piece, width),
            buffer(KINDS, CORES * width, width),
            buffer(CORES, *block),
            buffer(CORES, *block),
            buffer(CORES, *block),
            buffer(CORES, *block),
            buffer(KINDS, *block),
            buffer(KINDS, chips, piece, width),
            buffer(rows, KINDS, piece, width),
            dma((owned + 8,)),
            dma((3, chips)),
            dma((3, chips)),
            dma((2, chips)),
            dma((2, chips)),
            dma((2,)),
            dma((2,)),
            dma((KINDS, rows)),
            dma((KINDS, rows)),
            dma((rows + KINDS, chips, 2 * chips)),
            dma((rows, chips, 2)),
            dma((2, rows, owned)),
            dma((rows, owned)),
            dma((rows, owned)),
            dma((rows, owned)),
            dma((2,)),
            dma((2,)),
            dma((2,)),
            dma((len(STRIPS), chips)),
            dma((len(STRIPS), chips)),
            dma((2, len(STRIPS), rows, rows)),
            dma((len(STRIPS), rows)),
            dma((len(STRIPS), rows)),
            dma((len(STRIPS), chips)),
            dma((len(STRIPS),)),
        ],
        compiler_params=pltpu.CompilerParams(collective_id=0, has_side_effects=True),
    )(pattern_one.T, parents, anc_inverse, low_one, pivot_one, low_two, second_scaled_factor, second_pivot_inverse)
    return tuple(
        pl.pallas_call(
            finish_kernel,
            out_shape=[
                f32(CORES, *block),
                f32(1, *block),
                f32(CORES, *block),
                f32(1, *block),
                f32(1, *block),
            ],
            in_specs=[vmem] * 3,
            out_specs=[anywhere] * 5,
            scratch_shapes=[dma((5,))],
        )(
            *[
                pltpu.with_memory_space_constraint(x, pltpu.VMEM)
                for x in (column_one, column_two, final)
            ]
        )
    )


def solution(mesh):
    placed = (
        P("pcol", "prow"),
        P(),
        P(),
        P("pcol", "prow", None),
        P("pcol", None, None),
        P("pcol", "prow", None),
        P("pcol", None, None),
        P("pcol", None, None),
    )
    return jax.shard_map(
        body,
        mesh=mesh,
        in_specs=placed,
        out_specs=(
            P("prow", "pcol", None),
            P("pcol", None, None),
            P("prow", "pcol", None),
            P("pcol", None, None),
            P("pcol", None, None),
        ),
        check_vma=False,
    )
```

```python
import functools

import jax
import jax.numpy as jnp
from jax import lax
from jax.experimental import pallas as pl
from jax.experimental.pallas import tpu as pltpu
from jax.sharding import PartitionSpec as P

MESH = pl.DeviceIdType.MESH
CORES = 2
UP, DOWN = 0, 1
LOW_ONE, LOW_TWO, LOW_PARENT = 0, 1, 2
DIAG, CROSS, SECOND = 0, 1, 2
KINDS = 3
PARTS = 1
STRIPS = [(kind, part) for kind in range(KINDS) for part in range(PARTS)]


def split(x):
    hi = x.astype(jnp.bfloat16)
    return hi, (x - hi.astype(jnp.float32)).astype(jnp.bfloat16)


def dot3(left, right, transposed=False):
    contract = (((0,), (0,)), ((), ())) if transposed else (((1,), (0,)), ((), ()))
    dot = functools.partial(
        lax.dot_general, dimension_numbers=contract, preferred_element_type=jnp.float32
    )
    return dot(left[0], right[1]) + dot(left[1], right[0]) + dot(left[0], right[0])


def fused_kernel(
    rows,
    cols,
    pattern_table,
    parents_table,
    anc,
    low_one,
    pivot_one,
    low_two,
    factor,
    pivot_two,
    out_one,
    out_two,
    final,
    pattern,
    parents,
    z,
    low,
    whole_factor,
    pivot_own,
    pivot_second,
    scattered,
    scattered_pivot,
    scattered_two,
    staged,
    sums,
    column,
    parent_column,
    product,
    column_two,
    partial,
    partials,
    reduced,
    load_sem,
    scatter_send,
    scatter_recv,
    factor_send,
    factor_recv,
    swap_send,
    swap_recv,
    low_send,
    low_recv,
    share_send,
    share_recv,
    z_send,
    z_recv,
    near_send,
    near_recv,
    column_send,
    column_recv,
    column_store,
    part_send,
    part_recv,
    line_send,
    line_recv,
    last_send,
    last_recv,
    keep_sem,
):
    row, col = lax.axis_index("prow"), lax.axis_index("pcol")
    chips = cols // CORES
    width = factor.shape[1]
    piece = width // chips
    owned = anc.shape[1] // width
    chip, core = col // CORES, lax.rem(col, CORES)
    other = 1 - core
    mine = row * CORES + core
    partner = (row, chip * CORES + other)

    def beside(p):
        return (row, p * CORES + core)

    def turn(start, d, size):
        return lax.rem(start + d + size, size)

    def rows_of(p):
        return pl.ds(pl.multiple_of(p * piece, piece), piece)

    strip = piece // PARTS

    def strip_of(p, part):
        return pl.ds(pl.multiple_of(p * piece + part * strip, strip), strip)

    def remote(source, target, send, recv, device):
        return pltpu.make_async_remote_copy(
            src_ref=source,
            dst_ref=target,
            send_sem=send,
            recv_sem=recv,
            device_id=device,
            device_id_type=MESH,
        )

    def order(t):
        below, above = row, rows - 1 - row
        both = 2 * jnp.minimum(below, above)
        paired = t <= both
        distance = jnp.where(paired, (t + 1) // 2, t - both // 2)
        up = jnp.where(paired, lax.rem(t, 2) == 1, above > below)
        return jnp.where(up, row + distance, row - distance)

    sent = []

    loads = [
        pltpu.make_async_copy(
            anc.at[:, pl.ds(b * width, width)], z.at[row, core, b], load_sem.at[b]
        )
        for b in range(owned)
    ]
    loads_low = [
        pltpu.make_async_copy(
            low_one.at[0, rows_of(chip)], scattered.at[core, chip], load_sem.at[owned]
        ),
        pltpu.make_async_copy(
            low_two.at[0, rows_of(chip)], scattered_two.at[chip], load_sem.at[owned + 1]
        ),
        pltpu.make_async_copy(
            pivot_one.at[0, rows_of(chip)], scattered_pivot.at[core, chip], load_sem.at[owned + 2]
        ),
    ]
    loads_pivot = [
        pltpu.make_async_copy(pivot_one.at[0], pivot_own, load_sem.at[owned + 6]),
        pltpu.make_async_copy(pivot_two.at[0], pivot_second, load_sem.at[owned + 7]),
    ]
    load_factor = pltpu.make_async_copy(factor.at[0], whole_factor, load_sem.at[owned + 3])
    loads_index = [
        pltpu.make_async_copy(pattern_table, pattern, load_sem.at[owned + 4]),
        pltpu.make_async_copy(parents_table, parents, load_sem.at[owned + 5]),
    ]
    for copy in loads_index + loads + loads_low + loads_pivot:
        copy.start()

    @pl.when(chip == row)
    def _():
        load_factor.start()

    barrier = pltpu.get_barrier_semaphore()
    peers = [(turn(row, d, rows), col) for d in range(1, rows)]
    peers += [beside(turn(chip, d, chips)) for d in range(1, chips)] + [partner]
    for device in peers:
        pl.semaphore_signal(barrier, inc=1, device_id=device, device_id_type=MESH)
    pl.semaphore_wait(barrier, len(peers))

    def scatter(op, d, source, target, device):
        return remote(source, target, scatter_send.at[op, d], scatter_recv.at[op, d], device)

    scatters = [
        (low_one, scattered.at[core]),
        (low_two, scattered_two),
        (pivot_one, scattered_pivot.at[core]),
    ]
    swapped = [scattered, scattered_pivot]

    def scatter_all(op):
        source, target = scatters[op]
        for d in range(1, chips):
            p = turn(chip, d, chips)
            copy = scatter(op, d, source.at[0, rows_of(p)], target.at[chip], beside(p))
            copy.start()
            sent.append(copy)


    def z_line(source, b, direction):
        there = row + 1 if direction == UP else row - 1
        return remote(
            z.at[source, core, b],
            z.at[source, core, b],
            z_send.at[direction, source, b],
            z_recv.at[source, b],
            (there, col),
        )

    def z_near(source, b):
        return remote(
            z.at[source, core, b],
            z.at[source, core, b],
            near_send.at[source, b],
            near_recv.at[source, b],
            partner,
        )

    def z_near_arrival(source, b):
        target = z.at[source, other, b]
        return remote(target, target, near_send.at[source, b], near_recv.at[source, b], partner)

    def z_pass_on(source, b):
        @pl.when(jnp.logical_and(source <= row, row + 1 < rows))
        def _():
            z_line(source, b, UP).start()

        @pl.when(jnp.logical_and(source >= row, row > 0))
        def _():
            z_line(source, b, DOWN).start()

    def z_arrive(source, b):
        z_line(source, b, UP).wait_recv()
        z_pass_on(source, b)
        z_near(source, b).start()

    for b, copy in enumerate(loads):
        copy.wait()
        z_pass_on(row, b)

    scatter_all(0)
    scatter_all(1)
    for b in range(owned):
        z_near(row, b).start()

    def factor_piece(d, part, p):
        return remote(
            whole_factor.at[rows_of(part)],
            whole_factor.at[rows_of(part)],
            factor_send.at[0, d],
            factor_recv.at[0, d],
            beside(p),
        )

    def factor_first(d, p):
        return remote(
            factor.at[0, rows_of(p)],
            whole_factor.at[rows_of(p)],
            factor_send.at[1, d],
            factor_recv.at[1, 0],
            beside(p),
        )

    def arrivals(op, target):
        for d in range(1, chips):
            p = turn(chip, -d, chips)
            scatter(op, d, target.at[p], target.at[p], beside(p)).wait_recv()

    def swap(op):
        return remote(
            swapped[op].at[core],
            swapped[op].at[core],
            swap_send.at[op],
            swap_recv.at[op],
            partner,
        )

    def swap_arrival(op):
        return remote(
            swapped[op].at[other],
            swapped[op].at[other],
            swap_send.at[op],
            swap_recv.at[op],
            partner,
        )

    for copy in loads_low + loads_index:
        copy.wait()
    scatter_all(2)
    arrivals(0, scatters[0][1])
    swap(0).start()
    sent.append(swap(0))
    arrivals(1, scattered_two)
    swap_arrival(0).wait_recv()
    for plane in range(rows):
        parent = parents[plane * CORES + core]
        staged[plane] = scattered[lax.rem(parent, CORES), parent // CORES]

    def pieces_for(plane):
        return [scattered.at[core, plane], scattered_two.at[plane], staged.at[plane]]

    sources = [order(t) for t in range(rows)]
    for plane in sources[1:]:
        e = lax.rem(plane - row + rows, rows)
        for kind, source in enumerate(pieces_for(plane)):
            copy = remote(
                source,
                low.at[row, kind, rows_of(chip)],
                low_send.at[kind, e],
                low_recv.at[kind, e],
                (plane, col),
            )
            copy.start()
            sent.append(copy)

    masks = [1 << n for n in range((chips - 1).bit_length())]
    trees = [masks, masks[::-1]]
    offsets = sorted(range(1, chips), key=lambda o: o.bit_count())

    def flip(p, offset):
        for mask in masks:
            if offset & mask:
                p = p + mask - 2 * mask * lax.rem(p // mask, 2)
        return p

    def half_of(p, half):
        size = piece // 2
        return pl.ds(pl.multiple_of(p * piece + half * size, size), size)

    def share(source, offset, at, part, to, half):
        e = lax.rem(row - source + rows, rows)
        target = low.at[source, :, part]
        return remote(
            target, target, share_send.at[e, offset, at], share_recv.at[e, to, half], beside(flip(chip, offset))
        )

    def own_share(kind, source, mask):
        return remote(
            source,
            low.at[row, kind, rows_of(chip)],
            share_send.at[rows + kind, mask, 0],
            share_recv.at[0, mask, 0],
            beside(flip(chip, mask)),
        )

    def share_wait(source, offset, half):
        origin = flip(chip, offset)
        if offset not in masks:
            share(source, offset, 0, half_of(origin, half), offset, half).wait_recv()
        elif half == 0:
            share(source, offset, 0, rows_of(origin), offset, 0).wait_recv()

    def share_relay(source, last_hop):
        for offset in offsets:
            ways = [
                (half, tree[max(n for n, mask in enumerate(tree) if offset & mask) + 1 :])
                for half, tree in enumerate(trees)
            ]
            if last_hop != (not any(onward for _, onward in ways)):
                continue
            for half, onward in ways:
                share_wait(source, offset, half)
                for mask in onward:
                    copy = share(
                        source,
                        mask,
                        2 * offset + half,
                        half_of(flip(chip, offset), half),
                        offset ^ mask,
                        half,
                    )
                    copy.start()
                    sent.append(copy)

    def low_arrive(source):
        e = lax.rem(row - source + rows, rows)
        for kind in range(KINDS):
            target = low.at[source, kind, rows_of(chip)]
            remote(
                target, target, low_send.at[kind, e], low_recv.at[kind, e], (source, col)
            ).wait_recv()
        for mask in masks:
            copy = share(source, mask, 0, rows_of(chip), mask, 0)
            copy.start()
            sent.append(copy)

    for kind, source in enumerate(pieces_for(row)):
        for mask in masks:
            copy = own_share(kind, source, mask)
            copy.start()
            sent.append(copy)
    low[row, LOW_ONE, rows_of(chip)] = scattered[core, row]
    low[row, LOW_TWO, rows_of(chip)] = scattered_two[row]
    low[row, LOW_PARENT, rows_of(chip)] = staged[row]

    parent = parents[mine]

    def chosen(source, at):
        value = z[source, :, 0]
        for b in range(1, owned):
            value = jnp.where(at == b, z[source, :, b], value)
        return value.reshape(CORES * width, width)

    def store_column(at, buffer, out):
        keep = pltpu.make_async_copy(buffer.at[core], out.at[core], column_store.at[at])
        away = remote(
            buffer.at[other], out.at[core], column_send.at[at], column_recv.at[at], partner
        )
        keep.start()
        away.start()
        return keep, away

    def part_copy(kind, part, d, p, source, target):
        n = kind * PARTS + part
        return remote(source, target, part_send.at[n, d], part_recv.at[n, d], beside(p))

    def reduce_scatter(kind):
        for part in range(PARTS):
            for d in range(1, chips):
                p = turn(chip, d, chips)
                target = partials.at[kind, chip, strip_of(0, part)]
                copy = part_copy(kind, part, d, p, partial.at[kind, strip_of(p, part)], target)
                copy.start()
                sent.append(copy)

    slot_one = lax.rem(pattern[chip, mine], owned)
    slot_two = lax.rem(pattern[chip, parent], owned)
    stores = []

    def add_products(source, first_time=False, last_time=False):
        for b in range(owned):
            z_near_arrival(source, b).wait_recv()
        lhs = split(chosen(source, lax.rem(pattern[source, mine], owned)))
        first = dot3(lhs, split(low[source, LOW_ONE]))
        sums[0] = first if first_time else sums[0] + first
        if last_time:
            column[...] = -sums[0].reshape(CORES, width, width)
            partial[DIAG] = dot3(
                split(low[chip, LOW_ONE]), split(column[slot_one]), transposed=True
            )
            reduce_scatter(DIAG)
            stores.append(store_column(0, column, out_one))
        lhs = split(chosen(source, lax.rem(pattern[source, parent], owned)))
        second = dot3(lhs, split(low[source, LOW_PARENT]))
        third = dot3(lhs, split(low[source, LOW_TWO]))
        for n, value in enumerate([second, third], 1):
            sums[n] = value if first_time else sums[n] + value

    @pl.when(chip == row)
    def _():
        load_factor.wait()
        for d in range(1, chips):
            p = turn(chip, d, chips)
            factor_first(d, p).start()
            factor_piece(d, chip, p).start()

    inner = jnp.logical_and(row > 0, row + 1 < rows)

    @pl.when(inner)
    def _():
        for b in range(owned):
            for source in sources[1:3]:
                z_arrive(source, b)

    @pl.when(jnp.logical_not(inner))
    def _():
        for b in range(owned):
            z_arrive(sources[1], b)

    share_relay(row, False)
    low_arrive(sources[1])
    low_arrive(sources[2])
    share_relay(sources[1], False)
    for source in sources[3:]:
        low_arrive(source)
    @pl.when(inner)
    def _():
        for source in sources[3:]:
            z_arrive(source, 0)

    for source in sources[2:]:
        share_relay(source, False)

    @pl.when(inner)
    def _():
        for source in sources[3:]:
            for b in range(1, owned):
                z_arrive(source, b)

    @pl.when(chip != row)
    def _():
        factor_first(0, chip).wait_recv()
        for d in range(1, chips):
            p = turn(chip, d, chips)

            @pl.when(p != row)
            def _():
                factor_piece(d, chip, p).start()

    arrivals(2, scatters[2][1])
    swap(1).start()
    sent.append(swap(1))
    share_relay(row, True)
    add_products(row, True)
    share_relay(sources[1], True)
    add_products(sources[1])
    for source in sources[2:]:
        share_relay(source, True)

        @pl.when(jnp.logical_not(inner))
        def _():
            for b in range(owned):
                z_arrive(source, b)

        add_products(source, last_time=source is sources[-1])

    @pl.when(chip != row)
    def _():
        for d in range(1, chips):
            factor_piece(d, turn(chip, -d, chips), partner[1]).wait_recv()


    swap_arrival(1).wait_recv()
    whole = split(whole_factor[...])
    parent_column[...] = -sums[1].reshape(CORES, width, width)
    scaled = dot3(split(-sums[1]), whole)
    product[...] = scaled.reshape(CORES, width, width)
    column_two[...] = -(scaled + sums[2]).reshape(CORES, width, width)
    two_split = split(low[chip, LOW_TWO])
    cross = dot3(split(low[chip, LOW_PARENT]), split(product[slot_two]), transposed=True)
    cross = cross - dot3(split(parent_column[slot_two]), two_split, transposed=True)
    partial[CROSS] = cross
    pivot_rows = scattered_pivot[lax.rem(parent, CORES), parent // CORES]
    partial[CROSS, rows_of(chip)] -= dot3(split(pivot_rows), whole)
    stores.append(store_column(1, column_two, out_two))
    reduce_scatter(CROSS)
    partial[SECOND] = dot3(two_split, split(column_two[slot_two]), transposed=True) + dot3(
        whole, split(partial[CROSS]), transposed=True
    )
    reduce_scatter(SECOND)

    def line(kind, part, source, distance):
        way = UP if distance > 0 else DOWN
        n = kind * PARTS + part
        block = reduced.at[source, kind, strip_of(0, part)]
        return remote(
            block,
            block,
            line_send.at[way, n, source, abs(distance) - 1],
            line_recv.at[n, source],
            (row + distance, col),
        )

    def own_onward(kind, act):
        for distance in range(1, rows, 2):

            @pl.when(row + distance < rows)
            def _():
                act(distance)

            @pl.when(row >= distance)
            def _():
                act(-distance)

    def relay_onward(kind, source, act):
        odd = lax.rem(row + source, 2) == 1

        @pl.when(jnp.logical_and(odd, jnp.logical_and(source < row, row + 1 < rows)))
        def _():
            act(1)

        @pl.when(jnp.logical_and(odd, jnp.logical_and(source > row, row > 0)))
        def _():
            act(-1)

    def last(kind, part, source):
        n = kind * PARTS + part
        d = lax.rem(source - chip + chips, chips)
        return remote(
            reduced.at[source, kind, strip_of(0, part)],
            final.at[kind, strip_of(chip, part)],
            last_send.at[n, source],
            last_recv.at[n, d],
            beside(source),
        )

    def keep_sum(kind, part):
        return pltpu.make_async_copy(
            reduced.at[chip, kind, strip_of(0, part)],
            final.at[kind, strip_of(chip, part)],
            keep_sem.at[kind * PARTS + part],
        )

    def hand_on(kind, part, source):
        @pl.when(source != chip)
        def _():
            last(kind, part, source).start()

        @pl.when(source == chip)
        def _():
            keep_sum(kind, part).start()

    for kind, part in STRIPS:
        total = partial[kind, strip_of(chip, part)]
        for d in range(1, chips):
            p = turn(chip, -d, chips)
            target = partials.at[kind, p, strip_of(0, part)]
            part_copy(kind, part, d, p, target, target).wait_recv()
            total += partials[kind, p, strip_of(0, part)]
        reduced[row, kind, strip_of(0, part)] = total
        own_onward(kind, lambda distance: line(kind, part, row, distance).start())
        hand_on(kind, part, row)

    def spread(kind, part, source):
        @pl.when(source != row)
        def _():
            line(kind, part, source, 1).wait_recv()
            relay_onward(
                kind, source, lambda distance: line(kind, part, source, distance).start()
            )
            hand_on(kind, part, source)

    for source in range(1, rows - 1):
        for kind, part in STRIPS:
            spread(kind, part, source)
    near_end = jnp.where(2 * row < rows, 0, rows - 1)
    lag = PARTS
    for n in range(len(STRIPS) + lag):
        if n < len(STRIPS):
            spread(*STRIPS[n], near_end)
        if n >= lag:
            spread(*STRIPS[n - lag], rows - 1 - near_end)

    for keep, away in stores:
        keep.wait()
        away.wait_send()
        away.wait_recv()
    for copy in sent:
        copy.wait_send()

    @pl.when(chip == row)
    def _():
        for d in range(1, chips):
            p = turn(chip, d, chips)
            factor_first(d, p).wait_send()
            factor_piece(d, chip, p).wait_send()

    @pl.when(chip != row)
    def _():
        for d in range(1, chips):
            p = turn(chip, d, chips)

            @pl.when(p != row)
            def _():
                factor_piece(d, chip, p).wait_send()

    def drain(source, carry):
        for b in range(owned):
            z_near(source, b).wait_send()
        @pl.when(jnp.logical_and(source <= row, row + 1 < rows))
        def _():
            for b in range(owned):
                z_line(source, b, UP).wait_send()

        @pl.when(jnp.logical_and(source >= row, row > 0))
        def _():
            for b in range(owned):
                z_line(source, b, DOWN).wait_send()

        for kind, part in STRIPS:
            relay_onward(
                kind, source, lambda distance: line(kind, part, source, distance).wait_send()
            )

        @pl.when(source != chip)
        def _():
            for kind, part in STRIPS:
                last(kind, part, source).wait_send()

        return carry

    lax.fori_loop(0, rows, drain, 0)
    for kind, part in STRIPS:
        own_onward(kind, lambda distance: line(kind, part, row, distance).wait_send())

    for copy in loads_pivot:
        copy.wait()
    for kind, part in STRIPS:
        keep_sum(kind, part).wait()
        for d in range(1, chips):
            p = turn(chip, -d, chips)
            target = final.at[kind, strip_of(p, part)]
            n = kind * PARTS + part
            remote(
                target, target, last_send.at[n, 0], last_recv.at[n, d], beside(p)
            ).wait_recv()
        if part == PARTS - 1 and kind in (DIAG, SECOND):
            pivot = pivot_own if kind == DIAG else pivot_second
            final[kind] = pivot[...] - final[kind]


def finish_kernel(
    column_one, column_two, final, out_one, out_diag, out_two, out_cross, out_second, store_sem
):
    kept = [(column_one, out_one), (column_two, out_two), (final.at[DIAG], out_diag.at[0])]
    kept += [(final.at[CROSS], out_cross.at[0]), (final.at[SECOND], out_second.at[0])]
    stores = [
        pltpu.make_async_copy(place, out, store_sem.at[n]) for n, (place, out) in enumerate(kept)
    ]
    for copy in stores:
        copy.start()
    for copy in stores:
        copy.wait()


def body(
    anc_inverse,
    pattern_one,
    parents,
    low_one,
    pivot_one,
    low_two,
    second_scaled_factor,
    second_pivot_inverse,
):
    rows, cols = lax.axis_size("prow"), lax.axis_size("pcol")
    width = pivot_one.shape[1]
    chips = cols // CORES
    owned = anc_inverse.shape[1] // width
    piece = width // chips
    if rows != chips:
        raise ValueError("mesh shape")
    anywhere = pl.BlockSpec(memory_space=pl.ANY)
    vmem = pl.BlockSpec(memory_space=pltpu.VMEM)

    def f32(*shape):
        return jax.ShapeDtypeStruct(shape, jnp.float32)

    def buffer(*shape):
        return pltpu.VMEM(shape, jnp.float32)

    dma = pltpu.SemaphoreType.DMA
    block = (width, width)
    column_one, column_two, final = pl.pallas_call(
        functools.partial(fused_kernel, rows, cols),
        out_shape=[buffer(CORES, *block), buffer(CORES, *block), buffer(KINDS, *block)],
        in_specs=[anywhere] * 8,
        out_specs=[vmem, vmem, vmem],
        scratch_shapes=[
            pltpu.SMEM(pattern_one.shape[::-1], jnp.int32),
            pltpu.SMEM(parents.shape, jnp.int32),
            buffer(rows, CORES, owned, *block),
            buffer(rows, KINDS, *block),
            buffer(*block),
            buffer(*block),
            buffer(*block),
            buffer(CORES, chips, piece, width),
            buffer(CORES, chips, piece, width),
            buffer(chips, piece, width),
            buffer(rows, piece, width),
            buffer(KINDS, CORES * width, width),
            buffer(CORES, *block),
            buffer(CORES, *block),
            buffer(CORES, *block),
            buffer(CORES, *block),
            buffer(KINDS, *block),
            buffer(KINDS, chips, piece, width),
            buffer(rows, KINDS, piece, width),
            dma((owned + 8,)),
            dma((3, chips)),
            dma((3, chips)),
            dma((2, chips)),
            dma((2, chips)),
            dma((2,)),
            dma((2,)),
            dma((KINDS, rows)),
            dma((KINDS, rows)),
            dma((rows + KINDS, chips, 2 * chips)),
            dma((rows, chips, 2)),
            dma((2, rows, owned)),
            dma((rows, owned)),
            dma((rows, owned)),
            dma((rows, owned)),
            dma((2,)),
            dma((2,)),
            dma((2,)),
            dma((len(STRIPS), chips)),
            dma((len(STRIPS), chips)),
            dma((2, len(STRIPS), rows, rows)),
            dma((len(STRIPS), rows)),
            dma((len(STRIPS), rows)),
            dma((len(STRIPS), chips)),
            dma((len(STRIPS),)),
        ],
        compiler_params=pltpu.CompilerParams(collective_id=0, has_side_effects=True),
    )(pattern_one.T, parents, anc_inverse, low_one, pivot_one, low_two, second_scaled_factor, second_pivot_inverse)
    return tuple(
        pl.pallas_call(
            finish_kernel,
            out_shape=[
                f32(CORES, *block),
                f32(1, *block),
                f32(CORES, *block),
                f32(1, *block),
                f32(1, *block),
            ],
            in_specs=[vmem] * 3,
            out_specs=[anywhere] * 5,
            scratch_shapes=[dma((5,))],
        )(
            *[
                pltpu.with_memory_space_constraint(x, pltpu.VMEM)
                for x in (column_one, column_two, final)
            ]
        )
    )


def solution(mesh):
    placed = (
        P("pcol", "prow"),
        P(),
        P(),
        P("pcol", "prow", None),
        P("pcol", None, None),
        P("pcol", "prow", None),
        P("pcol", None, None),
        P("pcol", None, None),
    )
    return jax.shard_map(
        body,
        mesh=mesh,
        in_specs=placed,
        out_specs=(
            P("prow", "pcol", None),
            P("pcol", None, None),
            P("prow", "pcol", None),
            P("pcol", None, None),
            P("pcol", None, None),
        ),
        check_vma=False,
    )
```

```python
import functools

import jax
import jax.numpy as jnp
from jax import lax
from jax.experimental import pallas as pl
from jax.experimental.pallas import tpu as pltpu
from jax.sharding import PartitionSpec as P

MESH = pl.DeviceIdType.MESH
CORES = 2
UP, DOWN = 0, 1
LOW_ONE, LOW_TWO, LOW_PARENT = 0, 1, 2
DIAG, CROSS, SECOND = 0, 1, 2
KINDS = 3
PARTS = 1
STRIPS = [(kind, part) for kind in range(KINDS) for part in range(PARTS)]


def split(x):
    hi = x.astype(jnp.bfloat16)
    return hi, (x - hi.astype(jnp.float32)).astype(jnp.bfloat16)


def dot3(left, right, transposed=False):
    contract = (((0,), (0,)), ((), ())) if transposed else (((1,), (0,)), ((), ()))
    dot = functools.partial(
        lax.dot_general, dimension_numbers=contract, preferred_element_type=jnp.float32
    )
    return dot(left[0], right[1]) + dot(left[1], right[0]) + dot(left[0], right[0])


def fused_kernel(
    rows,
    cols,
    pattern_table,
    parents_table,
    anc,
    low_one,
    pivot_one,
    low_two,
    factor,
    pivot_two,
    out_one,
    out_two,
    final,
    pattern,
    parents,
    z,
    low,
    whole_factor,
    pivot_own,
    pivot_second,
    scattered,
    scattered_pivot,
    scattered_two,
    staged,
    sums,
    column,
    parent_column,
    product,
    column_two,
    partial,
    partials,
    reduced,
    load_sem,
    scatter_send,
    scatter_recv,
    factor_send,
    factor_recv,
    swap_send,
    swap_recv,
    low_send,
    low_recv,
    share_send,
    share_recv,
    z_send,
    z_recv,
    near_send,
    near_recv,
    column_send,
    column_recv,
    column_store,
    part_send,
    part_recv,
    line_send,
    line_recv,
    last_send,
    last_recv,
    keep_sem,
):
    row, col = lax.axis_index("prow"), lax.axis_index("pcol")
    chips = cols // CORES
    width = factor.shape[1]
    piece = width // chips
    owned = anc.shape[1] // width
    chip, core = col // CORES, lax.rem(col, CORES)
    other = 1 - core
    mine = row * CORES + core
    partner = (row, chip * CORES + other)

    def beside(p):
        return (row, p * CORES + core)

    def turn(start, d, size):
        return lax.rem(start + d + size, size)

    def rows_of(p):
        return pl.ds(pl.multiple_of(p * piece, piece), piece)

    strip = piece // PARTS

    def strip_of(p, part):
        return pl.ds(pl.multiple_of(p * piece + part * strip, strip), strip)

    def remote(source, target, send, recv, device):
        return pltpu.make_async_remote_copy(
            src_ref=source,
            dst_ref=target,
            send_sem=send,
            recv_sem=recv,
            device_id=device,
            device_id_type=MESH,
        )

    def order(t):
        below, above = row, rows - 1 - row
        both = 2 * jnp.minimum(below, above)
        paired = t <= both
        distance = jnp.where(paired, (t + 1) // 2, t - both // 2)
        up = jnp.where(paired, lax.rem(t, 2) == 1, above > below)
        return jnp.where(up, row + distance, row - distance)

    sent = []

    loads = [
        pltpu.make_async_copy(
            anc.at[:, pl.ds(b * width, width)], z.at[row, core, b], load_sem.at[b]
        )
        for b in range(owned)
    ]
    loads_low = [
        pltpu.make_async_copy(
            low_one.at[0, rows_of(chip)], scattered.at[core, chip], load_sem.at[owned]
        ),
        pltpu.make_async_copy(
            low_two.at[0, rows_of(chip)], scattered_two.at[chip], load_sem.at[owned + 1]
        ),
        pltpu.make_async_copy(
            pivot_one.at[0, rows_of(chip)], scattered_pivot.at[core, chip], load_sem.at[owned + 2]
        ),
    ]
    loads_pivot = [
        pltpu.make_async_copy(pivot_one.at[0], pivot_own, load_sem.at[owned + 6]),
        pltpu.make_async_copy(pivot_two.at[0], pivot_second, load_sem.at[owned + 7]),
    ]
    load_factor = pltpu.make_async_copy(factor.at[0], whole_factor, load_sem.at[owned + 3])
    loads_index = [
        pltpu.make_async_copy(pattern_table, pattern, load_sem.at[owned + 4]),
        pltpu.make_async_copy(parents_table, parents, load_sem.at[owned + 5]),
    ]
    for copy in loads_index + loads + loads_low + loads_pivot:
        copy.start()

    @pl.when(chip == row)
    def _():
        load_factor.start()

    barrier = pltpu.get_barrier_semaphore()
    peers = [(turn(row, d, rows), col) for d in range(1, rows)]
    peers += [beside(turn(chip, d, chips)) for d in range(1, chips)] + [partner]
    for device in peers:
        pl.semaphore_signal(barrier, inc=1, device_id=device, device_id_type=MESH)
    pl.semaphore_wait(barrier, len(peers))

    def scatter(op, d, source, target, device):
        return remote(source, target, scatter_send.at[op, d], scatter_recv.at[op, d], device)

    scatters = [
        (low_one, scattered.at[core]),
        (low_two, scattered_two),
        (pivot_one, scattered_pivot.at[core]),
    ]
    swapped = [scattered, scattered_pivot]

    def scatter_all(op):
        source, target = scatters[op]
        for d in range(1, chips):
            p = turn(chip, d, chips)
            copy = scatter(op, d, source.at[0, rows_of(p)], target.at[chip], beside(p))
            copy.start()
            sent.append(copy)


    def z_line(source, b, direction):
        there = row + 1 if direction == UP else row - 1
        return remote(
            z.at[source, core, b],
            z.at[source, core, b],
            z_send.at[direction, source, b],
            z_recv.at[source, b],
            (there, col),
        )

    def z_near(source, b):
        return remote(
            z.at[source, core, b],
            z.at[source, core, b],
            near_send.at[source, b],
            near_recv.at[source, b],
            partner,
        )

    def z_near_arrival(source, b):
        target = z.at[source, other, b]
        return remote(target, target, near_send.at[source, b], near_recv.at[source, b], partner)

    def z_pass_on(source, b):
        @pl.when(jnp.logical_and(source <= row, row + 1 < rows))
        def _():
            z_line(source, b, UP).start()

        @pl.when(jnp.logical_and(source >= row, row > 0))
        def _():
            z_line(source, b, DOWN).start()

    def z_arrive(source, b):
        z_line(source, b, UP).wait_recv()
        z_pass_on(source, b)
        z_near(source, b).start()

    for b, copy in enumerate(loads):
        copy.wait()
        z_pass_on(row, b)

    scatter_all(0)
    scatter_all(1)
    for b in range(owned):
        z_near(row, b).start()

    def factor_piece(d, part, p):
        return remote(
            whole_factor.at[rows_of(part)],
            whole_factor.at[rows_of(part)],
            factor_send.at[0, d],
            factor_recv.at[0, d],
            beside(p),
        )

    def factor_first(d, p):
        return remote(
            factor.at[0, rows_of(p)],
            whole_factor.at[rows_of(p)],
            factor_send.at[1, d],
            factor_recv.at[1, 0],
            beside(p),
        )

    def arrivals(op, target):
        for d in range(1, chips):
            p = turn(chip, -d, chips)
            scatter(op, d, target.at[p], target.at[p], beside(p)).wait_recv()

    def swap(op):
        return remote(
            swapped[op].at[core],
            swapped[op].at[core],
            swap_send.at[op],
            swap_recv.at[op],
            partner,
        )

    def swap_arrival(op):
        return remote(
            swapped[op].at[other],
            swapped[op].at[other],
            swap_send.at[op],
            swap_recv.at[op],
            partner,
        )

    for copy in loads_low + loads_index:
        copy.wait()
    scatter_all(2)
    arrivals(0, scatters[0][1])
    swap(0).start()
    sent.append(swap(0))
    arrivals(1, scattered_two)
    swap_arrival(0).wait_recv()
    for plane in range(rows):
        parent = parents[plane * CORES + core]
        staged[plane] = scattered[lax.rem(parent, CORES), parent // CORES]

    def pieces_for(plane):
        return [scattered.at[core, plane], scattered_two.at[plane], staged.at[plane]]

    sources = [order(t) for t in range(rows)]
    for plane in sources[1:]:
        e = lax.rem(plane - row + rows, rows)
        for kind, source in enumerate(pieces_for(plane)):
            copy = remote(
                source,
                low.at[row, kind, rows_of(chip)],
                low_send.at[kind, e],
                low_recv.at[kind, e],
                (plane, col),
            )
            copy.start()
            sent.append(copy)

    masks = [1 << n for n in range((chips - 1).bit_length())]
    trees = [masks, masks[::-1]]
    offsets = sorted(range(1, chips), key=lambda o: o.bit_count())

    def flip(p, offset):
        for mask in masks:
            if offset & mask:
                p = p + mask - 2 * mask * lax.rem(p // mask, 2)
        return p

    def half_of(p, half):
        size = piece // 2
        return pl.ds(pl.multiple_of(p * piece + half * size, size), size)

    def share(source, offset, at, part, to, half):
        e = lax.rem(row - source + rows, rows)
        target = low.at[source, :, part]
        return remote(
            target, target, share_send.at[e, offset, at], share_recv.at[e, to, half], beside(flip(chip, offset))
        )

    def own_share(kind, source, mask):
        return remote(
            source,
            low.at[row, kind, rows_of(chip)],
            share_send.at[rows + kind, mask, 0],
            share_recv.at[0, mask, 0],
            beside(flip(chip, mask)),
        )

    def share_wait(source, offset, half):
        origin = flip(chip, offset)
        if offset not in masks:
            share(source, offset, 0, half_of(origin, half), offset, half).wait_recv()
        elif half == 0:
            share(source, offset, 0, rows_of(origin), offset, 0).wait_recv()

    def share_relay(source, last_hop):
        for offset in offsets:
            ways = [
                (half, tree[max(n for n, mask in enumerate(tree) if offset & mask) + 1 :])
                for half, tree in enumerate(trees)
            ]
            if last_hop != (not any(onward for _, onward in ways)):
                continue
            for half, onward in ways:
                share_wait(source, offset, half)
                for mask in onward:
                    copy = share(
                        source,
                        mask,
                        2 * offset + half,
                        half_of(flip(chip, offset), half),
                        offset ^ mask,
                        half,
                    )
                    copy.start()
                    sent.append(copy)

    def low_arrive(source):
        e = lax.rem(row - source + rows, rows)
        for kind in range(KINDS):
            target = low.at[source, kind, rows_of(chip)]
            remote(
                target, target, low_send.at[kind, e], low_recv.at[kind, e], (source, col)
            ).wait_recv()
        for mask in masks:
            copy = share(source, mask, 0, rows_of(chip), mask, 0)
            copy.start()
            sent.append(copy)

    for kind, source in enumerate(pieces_for(row)):
        for mask in masks:
            copy = own_share(kind, source, mask)
            copy.start()
            sent.append(copy)
    low[row, LOW_ONE, rows_of(chip)] = scattered[core, row]
    low[row, LOW_TWO, rows_of(chip)] = scattered_two[row]
    low[row, LOW_PARENT, rows_of(chip)] = staged[row]

    parent = parents[mine]

    def chosen(source, at):
        value = z[source, :, 0]
        for b in range(1, owned):
            value = jnp.where(at == b, z[source, :, b], value)
        return value.reshape(CORES * width, width)

    def store_column(at, buffer, out):
        keep = pltpu.make_async_copy(buffer.at[core], out.at[core], column_store.at[at])
        away = remote(
            buffer.at[other], out.at[core], column_send.at[at], column_recv.at[at], partner
        )
        keep.start()
        away.start()
        return keep, away

    def part_copy(kind, part, d, p, source, target):
        n = kind * PARTS + part
        return remote(source, target, part_send.at[n, d], part_recv.at[n, d], beside(p))

    def reduce_scatter(kind):
        for part in range(PARTS):
            for d in range(1, chips):
                p = turn(chip, d, chips)
                target = partials.at[kind, chip, strip_of(0, part)]
                copy = part_copy(kind, part, d, p, partial.at[kind, strip_of(p, part)], target)
                copy.start()
                sent.append(copy)

    slot_one = lax.rem(pattern[chip, mine], owned)
    slot_two = lax.rem(pattern[chip, parent], owned)
    stores = []

    def add_products(source, first_time=False, last_time=False):
        for b in range(owned):
            z_near_arrival(source, b).wait_recv()
        lhs = split(chosen(source, lax.rem(pattern[source, mine], owned)))
        first = dot3(lhs, split(low[source, LOW_ONE]))
        sums[0] = first if first_time else sums[0] + first
        if last_time:
            column[...] = -sums[0].reshape(CORES, width, width)
            partial[DIAG] = dot3(
                split(low[chip, LOW_ONE]), split(column[slot_one]), transposed=True
            )
            reduce_scatter(DIAG)
            stores.append(store_column(0, column, out_one))
        lhs = split(chosen(source, lax.rem(pattern[source, parent], owned)))
        second = dot3(lhs, split(low[source, LOW_PARENT]))
        third = dot3(lhs, split(low[source, LOW_TWO]))
        for n, value in enumerate([second, third], 1):
            sums[n] = value if first_time else sums[n] + value

    @pl.when(chip == row)
    def _():
        load_factor.wait()
        for d in range(1, chips):
            p = turn(chip, d, chips)
            factor_first(d, p).start()
            factor_piece(d, chip, p).start()

    inner = jnp.logical_and(row > 0, row + 1 < rows)

    @pl.when(inner)
    def _():
        for b in range(owned):
            for source in sources[1:3]:
                z_arrive(source, b)

    @pl.when(jnp.logical_not(inner))
    def _():
        for b in range(owned):
            z_arrive(sources[1], b)

    share_relay(row, False)
    low_arrive(sources[1])
    low_arrive(sources[2])
    share_relay(sources[1], False)
    for source in sources[3:]:
        low_arrive(source)
    @pl.when(inner)
    def _():
        for source in sources[3:]:
            z_arrive(source, 0)

    for source in sources[2:]:
        share_relay(source, False)

    @pl.when(inner)
    def _():
        for source in sources[3:]:
            for b in range(1, owned):
                z_arrive(source, b)

    @pl.when(chip != row)
    def _():
        factor_first(0, chip).wait_recv()
        for d in range(1, chips):
            p = turn(chip, d, chips)

            @pl.when(p != row)
            def _():
                factor_piece(d, chip, p).start()

    arrivals(2, scatters[2][1])
    swap(1).start()
    sent.append(swap(1))
    share_relay(row, True)
    add_products(row, True)
    share_relay(sources[1], True)
    add_products(sources[1])
    for source in sources[2:]:
        share_relay(source, True)

        @pl.when(jnp.logical_not(inner))
        def _():
            for b in range(owned):
                z_arrive(source, b)

        add_products(source, last_time=source is sources[-1])

    @pl.when(chip != row)
    def _():
        for d in range(1, chips):
            factor_piece(d, turn(chip, -d, chips), partner[1]).wait_recv()


    swap_arrival(1).wait_recv()
    whole = split(whole_factor[...])
    parent_column[...] = -sums[1].reshape(CORES, width, width)
    scaled = dot3(split(-sums[1]), whole)
    product[...] = scaled.reshape(CORES, width, width)
    two_split = split(low[chip, LOW_TWO])
    cross = dot3(split(low[chip, LOW_PARENT]), split(product[slot_two]), transposed=True)
    cross = cross - dot3(split(parent_column[slot_two]), two_split, transposed=True)
    partial[CROSS] = cross
    pivot_rows = scattered_pivot[lax.rem(parent, CORES), parent // CORES]
    partial[CROSS, rows_of(chip)] -= dot3(split(pivot_rows), whole)
    reduce_scatter(CROSS)
    column_two[...] = -(scaled + sums[2]).reshape(CORES, width, width)
    partial[SECOND] = dot3(two_split, split(column_two[slot_two]), transposed=True) + dot3(
        whole, split(partial[CROSS]), transposed=True
    )
    reduce_scatter(SECOND)
    stores.append(store_column(1, column_two, out_two))

    def line(kind, part, source, distance):
        way = UP if distance > 0 else DOWN
        n = kind * PARTS + part
        block = reduced.at[source, kind, strip_of(0, part)]
        return remote(
            block,
            block,
            line_send.at[way, n, source, abs(distance) - 1],
            line_recv.at[n, source],
            (row + distance, col),
        )

    def own_onward(kind, act):
        for distance in range(1, rows, 2):

            @pl.when(row + distance < rows)
            def _():
                act(distance)

            @pl.when(row >= distance)
            def _():
                act(-distance)

    def relay_onward(kind, source, act):
        odd = lax.rem(row + source, 2) == 1

        @pl.when(jnp.logical_and(odd, jnp.logical_and(source < row, row + 1 < rows)))
        def _():
            act(1)

        @pl.when(jnp.logical_and(odd, jnp.logical_and(source > row, row > 0)))
        def _():
            act(-1)

    def last(kind, part, source):
        n = kind * PARTS + part
        d = lax.rem(source - chip + chips, chips)
        return remote(
            reduced.at[source, kind, strip_of(0, part)],
            final.at[kind, strip_of(chip, part)],
            last_send.at[n, source],
            last_recv.at[n, d],
            beside(source),
        )

    def keep_sum(kind, part):
        return pltpu.make_async_copy(
            reduced.at[chip, kind, strip_of(0, part)],
            final.at[kind, strip_of(chip, part)],
            keep_sem.at[kind * PARTS + part],
        )

    def hand_on(kind, part, source):
        @pl.when(source != chip)
        def _():
            last(kind, part, source).start()

        @pl.when(source == chip)
        def _():
            keep_sum(kind, part).start()

    for kind, part in STRIPS:
        total = partial[kind, strip_of(chip, part)]
        for d in range(1, chips):
            p = turn(chip, -d, chips)
            target = partials.at[kind, p, strip_of(0, part)]
            part_copy(kind, part, d, p, target, target).wait_recv()
            total += partials[kind, p, strip_of(0, part)]
        reduced[row, kind, strip_of(0, part)] = total
        own_onward(kind, lambda distance: line(kind, part, row, distance).start())
        hand_on(kind, part, row)

    def spread(kind, part, source):
        @pl.when(source != row)
        def _():
            line(kind, part, source, 1).wait_recv()
            relay_onward(
                kind, source, lambda distance: line(kind, part, source, distance).start()
            )
            hand_on(kind, part, source)

    for source in range(1, rows - 1):
        for kind, part in STRIPS:
            spread(kind, part, source)
    near_end = jnp.where(2 * row < rows, 0, rows - 1)
    lag = PARTS
    for n in range(len(STRIPS) + lag):
        if n < len(STRIPS):
            spread(*STRIPS[n], near_end)
        if n >= lag:
            spread(*STRIPS[n - lag], rows - 1 - near_end)

    for keep, away in stores:
        keep.wait()
        away.wait_send()
        away.wait_recv()
    for copy in sent:
        copy.wait_send()

    @pl.when(chip == row)
    def _():
        for d in range(1, chips):
            p = turn(chip, d, chips)
            factor_first(d, p).wait_send()
            factor_piece(d, chip, p).wait_send()

    @pl.when(chip != row)
    def _():
        for d in range(1, chips):
            p = turn(chip, d, chips)

            @pl.when(p != row)
            def _():
                factor_piece(d, chip, p).wait_send()

    def drain(source, carry):
        for b in range(owned):
            z_near(source, b).wait_send()
        @pl.when(jnp.logical_and(source <= row, row + 1 < rows))
        def _():
            for b in range(owned):
                z_line(source, b, UP).wait_send()

        @pl.when(jnp.logical_and(source >= row, row > 0))
        def _():
            for b in range(owned):
                z_line(source, b, DOWN).wait_send()

        for kind, part in STRIPS:
            relay_onward(
                kind, source, lambda distance: line(kind, part, source, distance).wait_send()
            )

        @pl.when(source != chip)
        def _():
            for kind, part in STRIPS:
                last(kind, part, source).wait_send()

        return carry

    lax.fori_loop(0, rows, drain, 0)
    for kind, part in STRIPS:
        own_onward(kind, lambda distance: line(kind, part, row, distance).wait_send())

    for copy in loads_pivot:
        copy.wait()
    for kind, part in STRIPS:
        keep_sum(kind, part).wait()
        for d in range(1, chips):
            p = turn(chip, -d, chips)
            target = final.at[kind, strip_of(p, part)]
            n = kind * PARTS + part
            remote(
                target, target, last_send.at[n, 0], last_recv.at[n, d], beside(p)
            ).wait_recv()
        if part == PARTS - 1 and kind in (DIAG, SECOND):
            pivot = pivot_own if kind == DIAG else pivot_second
            final[kind] = pivot[...] - final[kind]


def finish_kernel(
    column_one, column_two, final, out_one, out_diag, out_two, out_cross, out_second, store_sem
):
    kept = [(column_one, out_one), (column_two, out_two), (final.at[DIAG], out_diag.at[0])]
    kept += [(final.at[CROSS], out_cross.at[0]), (final.at[SECOND], out_second.at[0])]
    stores = [
        pltpu.make_async_copy(place, out, store_sem.at[n]) for n, (place, out) in enumerate(kept)
    ]
    for copy in stores:
        copy.start()
    for copy in stores:
        copy.wait()


def body(
    anc_inverse,
    pattern_one,
    parents,
    low_one,
    pivot_one,
    low_two,
    second_scaled_factor,
    second_pivot_inverse,
):
    rows, cols = lax.axis_size("prow"), lax.axis_size("pcol")
    width = pivot_one.shape[1]
    chips = cols // CORES
    owned = anc_inverse.shape[1] // width
    piece = width // chips
    if rows != chips:
        raise ValueError("mesh shape")
    anywhere = pl.BlockSpec(memory_space=pl.ANY)
    vmem = pl.BlockSpec(memory_space=pltpu.VMEM)

    def f32(*shape):
        return jax.ShapeDtypeStruct(shape, jnp.float32)

    def buffer(*shape):
        return pltpu.VMEM(shape, jnp.float32)

    dma = pltpu.SemaphoreType.DMA
    block = (width, width)
    column_one, column_two, final = pl.pallas_call(
        functools.partial(fused_kernel, rows, cols),
        out_shape=[buffer(CORES, *block), buffer(CORES, *block), buffer(KINDS, *block)],
        in_specs=[anywhere] * 8,
        out_specs=[vmem, vmem, vmem],
        scratch_shapes=[
            pltpu.SMEM(pattern_one.shape[::-1], jnp.int32),
            pltpu.SMEM(parents.shape, jnp.int32),
            buffer(rows, CORES, owned, *block),
            buffer(rows, KINDS, *block),
            buffer(*block),
            buffer(*block),
            buffer(*block),
            buffer(CORES, chips, piece, width),
            buffer(CORES, chips, piece, width),
            buffer(chips, piece, width),
            buffer(rows, piece, width),
            buffer(KINDS, CORES * width, width),
            buffer(CORES, *block),
            buffer(CORES, *block),
            buffer(CORES, *block),
            buffer(CORES, *block),
            buffer(KINDS, *block),
            buffer(KINDS, chips, piece, width),
            buffer(rows, KINDS, piece, width),
            dma((owned + 8,)),
            dma((3, chips)),
            dma((3, chips)),
            dma((2, chips)),
            dma((2, chips)),
            dma((2,)),
            dma((2,)),
            dma((KINDS, rows)),
            dma((KINDS, rows)),
            dma((rows + KINDS, chips, 2 * chips)),
            dma((rows, chips, 2)),
            dma((2, rows, owned)),
            dma((rows, owned)),
            dma((rows, owned)),
            dma((rows, owned)),
            dma((2,)),
            dma((2,)),
            dma((2,)),
            dma((len(STRIPS), chips)),
            dma((len(STRIPS), chips)),
            dma((2, len(STRIPS), rows, rows)),
            dma((len(STRIPS), rows)),
            dma((len(STRIPS), rows)),
            dma((len(STRIPS), chips)),
            dma((len(STRIPS),)),
        ],
        compiler_params=pltpu.CompilerParams(collective_id=0, has_side_effects=True),
    )(pattern_one.T, parents, anc_inverse, low_one, pivot_one, low_two, second_scaled_factor, second_pivot_inverse)
    return tuple(
        pl.pallas_call(
            finish_kernel,
            out_shape=[
                f32(CORES, *block),
                f32(1, *block),
                f32(CORES, *block),
                f32(1, *block),
                f32(1, *block),
            ],
            in_specs=[vmem] * 3,
            out_specs=[anywhere] * 5,
            scratch_shapes=[dma((5,))],
        )(
            *[
                pltpu.with_memory_space_constraint(x, pltpu.VMEM)
                for x in (column_one, column_two, final)
            ]
        )
    )


def solution(mesh):
    placed = (
        P("pcol", "prow"),
        P(),
        P(),
        P("pcol", "prow", None),
        P("pcol", None, None),
        P("pcol", "prow", None),
        P("pcol", None, None),
        P("pcol", None, None),
    )
    return jax.shard_map(
        body,
        mesh=mesh,
        in_specs=placed,
        out_specs=(
            P("prow", "pcol", None),
            P("pcol", None, None),
            P("prow", "pcol", None),
            P("pcol", None, None),
            P("pcol", None, None),
        ),
        check_vma=False,
    )
```
